32 devices in a mesh: event: 2 (over x), phi: 16 (over z, y, core).
Axes of the slice: x: 2, y: 2, z: 4, core: 2. Of those that a mesh axis runs over, the one named last changes fastest.
Arguments:
- hit_feats: bfloat16 [12, 131072], P(None, ('event', 'phi')), parts along dimension 1, may hold values from -6 to 6
- layer_ids: int32 [131072], P(('event', 'phi')), parts along dimension 0, may hold values from 0 to 15
- edge_tiles: bfloat16 [1024, 8, 128, 128], P(('event', 'phi')), parts along dimension 0
- src_blocks: int32 [1024, 8], P(('event', 'phi')), parts along dimension 0, may hold values from 0 to 159
- live_slots: int32 [1024], P(('event', 'phi')), parts along dimension 0, may hold values from 1 to 8, as said below
- anchor_hits: int32 [32768], P(('event', 'phi')), parts along dimension 0, may hold values from 0 to 4095
- positive_hits: int32 [32768], P(('event', 'phi')), parts along dimension 0, may hold values from 0 to 20479
- negative_hits: int32 [32768], P(('event', 'phi')), parts along dimension 0, may hold values from 0 to 20479
- w_enc: bfloat16 [12, 128], replicated, may hold values from -1.75 to 1.75
- layer_table: bfloat16 [16, 128], replicated, may hold values from -3 to 3
- w_self: bfloat16 [2, 128, 128], replicated, may hold values from -0.5 to 0.5
- w_agg: bfloat16 [2, 128, 128], replicated, may hold values from -0.5 to 0.5
- w_out: bfloat16 [2, 128, 128], replicated, may hold values from -0.5 to 0.5
Outputs:
- loss: float32 [2], P('event'), parts along dimension 0
- grad_enc: float32 [24, 128], P('event'), parts along dimension 0
- grad_table: float32 [32, 128], P('event'), parts along dimension 0
- grad_self: float32 [4, 128, 128], P('event'), parts along dimension 0
- grad_agg: float32 [4, 128, 128], P('event'), parts along dimension 0
- grad_out: float32 [4, 128, 128], P('event'), parts along dimension 0
The draws below stay inside these ranges and needn't reach their ends.
There are 2 independent parts, one for each index of `event`. The reference program is written for one: setup_inputs(seed, part) draws one part's arguments, and reference() takes and returns one part's arrays. A program takes and returns all parts, laid end to end along the dimension named above; an argument that names none is the same for every part. Nothing has to cross between parts.
Inputs may be any that keep to these rules, and one draw needn't show every extreme that they name: `live_slots`: in every draw some node block has all 8 slots live.
All inputs are finite; a program needn't handle non-finite values.
Results may differ from the reference program's by a relative error of at most 0.0022.
Values may be sent and summed in bfloat16 or wider, within the bound.
A program may use at most 128 MiB of HBM per device.

```python
import math
import jax
import jax.numpy as jnp
from jax import lax

WIDTH = 128
FEAT = 12
NLAY = 16
LAYERS = 2
BLK = 128
SLOTS = 8
REACH = 2
NB = 32
CON = 1024
NB_ALL = 512
HITS = 65536
CON_ALL = 16384
N_PHI = 16


def draw_edge_tiles(key, part):
    first_key, second_key = jax.random.split(key)
    shape = (NB_ALL, SLOTS, BLK, BLK)
    present = jax.random.uniform(first_key, shape, jnp.float32) < 0.25
    weights = jax.random.uniform(second_key, shape, jnp.float32, minval=0.05, maxval=0.25)
    return jnp.where(present, weights, 0.0).astype(jnp.bfloat16)


def draw_live_slots(key, part):
    sector_count = NB_ALL // NB
    first_key, second_key, third_key = jax.random.split(key, 3)
    order = jax.random.permutation(first_key, sector_count).astype(jnp.int32)
    level = 1 + order * SLOTS // sector_count
    level_rows = jnp.repeat(level, NB)
    dropped = jax.random.randint(second_key, (NB_ALL,), 0, level_rows // 2 + 1, dtype=jnp.int32)
    counts = level_rows - dropped
    chosen_block = jax.random.randint(third_key, (sector_count,), 0, NB, dtype=jnp.int32)
    filled = jnp.arange(NB_ALL, dtype=jnp.int32) % NB == jnp.repeat(chosen_block, NB)
    return jnp.where(filled, level_rows, counts).astype(jnp.int32)


def set_ends(result, own_key, smallest, top_value):
    spot = [jax.random.randint(jax.random.fold_in(own_key, axis), (), 0, length) for axis, length in enumerate(result.shape)]
    main_axis = result.shape.index(max(result.shape))
    next_to = spot[:main_axis] + [(spot[main_axis] + 1) % result.shape[main_axis]] + spot[main_axis + 1:]
    return result.at[tuple(spot)].set(smallest).at[tuple(next_to)].set(top_value)


def level_of(key, extent, cuts, low, largest):
    level, own = 1.0, jax.random.fold_in(key, 6)
    for position, parts in cuts:
        draws = jnp.exp(jax.random.uniform(jax.random.fold_in(own, position), (parts,), jnp.float32, low / len(cuts), largest / len(cuts)))
        level = level * jnp.repeat(draws, extent[position] // parts).reshape([-1 if axis == position else 1 for axis in range(len(extent))])
    return level


def normal_values(key, dims, width, most, cuts=(), kind=jnp.bfloat16):
    values = jax.random.normal(key, dims, jnp.float32) * width
    if len(cuts) > 0:
        values = level_of(key, dims, cuts, -0.22, 0.18) * values
    return jnp.clip(values, min=-most, max=most).astype(kind)


def setup_inputs(seed: int = 0, part: int = 0) -> dict:
    splits = jax.random.split(jax.random.key(seed), 14)
    part_splits = jax.random.split(jax.random.fold_in(splits[13], part), 14)
    hit_feats = normal_values(part_splits[0], (FEAT, HITS), 1.0, 6.0, ((1, 16),))
    layer_ids = set_ends(jax.random.randint(part_splits[1], (HITS,), 0, NLAY), jax.random.fold_in(part_splits[1], 1), 0, NLAY - 1).astype(jnp.int32)
    edge_tiles = draw_edge_tiles(jax.random.fold_in(jax.random.fold_in(splits[13], part), 71), part)
    src_blocks = set_ends(jax.random.randint(part_splits[3], (NB_ALL, SLOTS), 0, (2 * REACH + 1) * NB), jax.random.fold_in(part_splits[3], 1), 0, ((2 * REACH + 1) * NB) - 1).astype(jnp.int32)
    live_slots = draw_live_slots(jax.random.fold_in(jax.random.fold_in(splits[13], part), 71), part)
    anchor_hits = set_ends(jax.random.randint(part_splits[5], (CON_ALL,), 0, NB * BLK), jax.random.fold_in(part_splits[5], 1), 0, (NB * BLK) - 1).astype(jnp.int32)
    positive_hits = set_ends(jax.random.randint(part_splits[6], (CON_ALL,), 0, (2 * REACH + 1) * NB * BLK), jax.random.fold_in(part_splits[6], 1), 0, ((2 * REACH + 1) * NB * BLK) - 1).astype(jnp.int32)
    negative_hits = set_ends(jax.random.randint(part_splits[7], (CON_ALL,), 0, (2 * REACH + 1) * NB * BLK), jax.random.fold_in(part_splits[7], 1), 0, ((2 * REACH + 1) * NB * BLK) - 1).astype(jnp.int32)
    w_enc = normal_values(splits[8], (FEAT, WIDTH), FEAT ** -0.5, 1.75)
    layer_table = normal_values(splits[9], (NLAY, WIDTH), 0.5, 3.0)
    w_self = normal_values(splits[10], (LAYERS, WIDTH, WIDTH), WIDTH ** -0.5, 0.5)
    w_agg = normal_values(splits[11], (LAYERS, WIDTH, WIDTH), WIDTH ** -0.5, 0.5)
    w_out = normal_values(splits[12], (LAYERS, WIDTH, WIDTH), WIDTH ** -0.5, 0.5)
    return {"hit_feats": hit_feats, "layer_ids": layer_ids, "edge_tiles": edge_tiles, "src_blocks": src_blocks, "live_slots": live_slots, "anchor_hits": anchor_hits, "positive_hits": positive_hits, "negative_hits": negative_hits, "w_enc": w_enc, "layer_table": layer_table, "w_self": w_self, "w_agg": w_agg, "w_out": w_out}


loss_divisor = 64.0

def contract_rows(left_side, right_side):
    return lax.dot_general(left_side, right_side, (((0,), (0,)), ((), ())), preferred_element_type=jnp.float32)

def contract_cols(left_side, right_side):
    return lax.dot_general(left_side, right_side, (((1,), (1,)), ((), ())), preferred_element_type=jnp.float32)

def contract_inner(left_side, right_side):
    return lax.dot_general(left_side, right_side, (((1,), (0,)), ((), ())), preferred_element_type=jnp.float32)

def contrast_terms(window, anchor_here, positive_here, negative_here, centre, latent_width):
    anchor = window[centre + anchor_here].astype(jnp.float32)
    positive = window[positive_here].astype(jnp.float32)
    negative = window[negative_here].astype(jnp.float32)
    inv_root = 1.0 / math.sqrt(latent_width)
    score_gap = (lax.optimization_barrier(jnp.sum(anchor * negative, axis=1)) - lax.optimization_barrier(jnp.sum(anchor * positive, axis=1))) * inv_root
    return (score_gap, anchor, positive, negative)

def contrast_grad(window, anchor_here, positive_here, negative_here, centre, latent_width):
    score_gap, anchor, positive, negative = contrast_terms(window, anchor_here, positive_here, negative_here, centre, latent_width)
    weight_coef = (jax.nn.sigmoid(score_gap) * (1.0 / (loss_divisor * math.sqrt(latent_width))))[:, None]
    gradient = jnp.zeros(window.shape, jnp.float32)
    gradient = gradient.at[centre + anchor_here].add(weight_coef * (negative - positive))
    gradient = gradient.at[positive_here].add(-weight_coef * anchor)
    gradient = gradient.at[negative_here].add(weight_coef * anchor)
    return gradient

def reference(hit_feats, layer_ids, edge_tiles, src_blocks, live_slots, anchor_hits, positive_hits, negative_hits, w_enc, layer_table, w_self, w_agg, w_out):
    hit_count = NB * BLK
    span_count = 2 * REACH + 1
    sectors = jnp.arange(N_PHI, dtype=jnp.int32)
    offsets = jnp.arange(-REACH, REACH + 1, dtype=jnp.int32)
    onehot = (jnp.arange(NLAY, dtype=jnp.int32)[:, None] == layer_ids[None, :]).astype(jnp.bfloat16)
    encoded = contract_rows(hit_feats, w_enc) + contract_rows(onehot, layer_table)
    squashed = jnp.tanh(encoded)
    latents = squashed.astype(jnp.bfloat16)
    tiles = edge_tiles.reshape(N_PHI, NB, SLOTS, BLK, BLK)
    sources = src_blocks.reshape(N_PHI, NB, SLOTS)
    live_mask = jnp.arange(SLOTS, dtype=jnp.int32)[None, None, :] < live_slots.reshape(N_PHI, NB)[:, :, None]

    def window_of(grid, sector):
        return jnp.take(grid, (sector + offsets) % N_PHI, axis=0).reshape(span_count * hit_count, WIDTH)

    def aggregate(current):
        grid = current.reshape(N_PHI, hit_count, WIDTH)

        def one_sector(sector_items):
            sector, tiles_here, sources_here, live_here = sector_items
            blocks = window_of(grid, sector).reshape(span_count * NB, BLK, WIDTH)
            chosen = jnp.where(live_here[:, :, None, None], blocks[sources_here], jnp.zeros((), blocks.dtype))
            return jnp.einsum('bsij,bsjw->biw', tiles_here.astype(jnp.float32), chosen.astype(jnp.float32))
        return lax.map(one_sector, (sectors, tiles, sources, live_mask)).reshape(N_PHI * hit_count, WIDTH)

    def give_back(piece_fn, sector_items):

        def advance(running, item_now):
            pieces = piece_fn(item_now).reshape(span_count, hit_count, WIDTH)
            for slot_index in range(span_count):
                portion = pieces[slot_index]
                if slot_index != REACH:
                    portion = lax.optimization_barrier(portion.astype(jnp.bfloat16)).astype(jnp.float32)
                target = (item_now[0] + slot_index - REACH) % N_PHI
                current = lax.dynamic_index_in_dim(running, target, 0, keepdims=False)
                running = lax.dynamic_update_index_in_dim(running, current + portion, target, 0)
            return (running, None)
        running, _ = lax.scan(advance, jnp.zeros((N_PHI, hit_count, WIDTH), jnp.float32), sector_items)
        return running.reshape(N_PHI * hit_count, WIDTH)
    stored = []
    for layer_index in range(LAYERS):
        aggregated = aggregate(latents).astype(jnp.bfloat16)
        activation = jnp.dot(latents, w_self[layer_index], preferred_element_type=jnp.float32) + jnp.dot(aggregated, w_agg[layer_index], preferred_element_type=jnp.float32)
        hidden = jax.nn.relu(activation).astype(jnp.bfloat16)
        updated = (latents.astype(jnp.float32) + jnp.dot(hidden, w_out[layer_index], preferred_element_type=jnp.float32)).astype(jnp.bfloat16)
        stored.append((latents, aggregated, activation, hidden))
        latents = updated
    final_grid = latents.reshape(N_PHI, hit_count, WIDTH)
    centre = REACH * hit_count
    triplets = (sectors, anchor_hits.reshape(N_PHI, CON), positive_hits.reshape(N_PHI, CON), negative_hits.reshape(N_PHI, CON))

    def sector_loss(sector_items):
        sector, anchor_here, positive_here, negative_here = sector_items
        score_gap = contrast_terms(window_of(final_grid, sector), anchor_here, positive_here, negative_here, centre, WIDTH)[0]
        return jnp.sum(jax.nn.softplus(score_gap))
    loss = (jnp.sum(lax.map(sector_loss, triplets)) / CON_ALL).reshape(1)

    def contrast_piece(sector_items):
        sector, anchor_here, positive_here, negative_here = sector_items
        return contrast_grad(window_of(final_grid, sector), anchor_here, positive_here, negative_here, centre, WIDTH)
    gradient = give_back(contrast_piece, triplets)
    self_grads = [None] * LAYERS
    agg_grads = [None] * LAYERS
    out_grads = [None] * LAYERS
    for layer_index in range(LAYERS - 1, -1, -1):
        before, aggregated, activation, hidden = stored[layer_index]
        upstream = gradient.astype(jnp.bfloat16)
        out_grads[layer_index] = contract_rows(hidden, upstream)
        hidden_grad = contract_cols(upstream, w_out[layer_index])
        act_grad = jnp.where(activation > 0, hidden_grad, 0.0).astype(jnp.bfloat16)
        self_grads[layer_index] = contract_rows(before, act_grad)
        agg_grads[layer_index] = contract_rows(aggregated, act_grad)
        agg_grad = contract_cols(act_grad, w_agg[layer_index]).astype(jnp.bfloat16)
        direct = gradient + contract_cols(act_grad, w_self[layer_index])
        agg_grid = agg_grad.reshape(N_PHI, NB, BLK, WIDTH)

        def adjacency_piece(sector_items):
            sector, tiles_here, sources_here, live_here, grad_here = sector_items
            contrib = jnp.einsum('bsij,biw->bsjw', tiles_here.astype(jnp.float32), grad_here.astype(jnp.float32))
            contrib = jnp.where(live_here[:, :, None, None], contrib, 0.0)
            return jax.ops.segment_sum(contrib.reshape(NB * SLOTS, BLK, WIDTH), sources_here.reshape(NB * SLOTS), num_segments=span_count * NB)
        gradient = direct + give_back(adjacency_piece, (sectors, tiles, sources, live_mask, agg_grid))
    encoded_grad = (gradient * (1.0 - squashed * squashed)).astype(jnp.bfloat16)
    grad_enc = contract_inner(hit_feats, encoded_grad)
    grad_table = contract_inner(onehot, encoded_grad)
    return (loss, grad_enc, grad_table, jnp.stack(self_grads), jnp.stack(agg_grads), jnp.stack(out_grads))
```

```python
import functools
import math

import jax
import jax.numpy as jnp
from jax import lax
from jax.experimental import pallas as pl
from jax.experimental.pallas import tpu as pltpu
from jax.sharding import PartitionSpec as P

loss_divisor = 64.0
F32 = jnp.float32
BF16 = jnp.bfloat16
VMEM_BYTES = 60 * 1024 * 1024


def dot(left, right, left_dim, right_dim):
    return lax.dot_general(
        left, right, (((left_dim,), (right_dim,)), ((), ())), preferred_element_type=F32
    )


def full(shape):
    return pl.BlockSpec(shape, lambda *_: (0,) * len(shape))


def params():
    return pltpu.CompilerParams(
        dimension_semantics=("arbitrary",), vmem_limit_bytes=VMEM_BYTES
    )


def permute_far(value, steps):
    count = lax.axis_size("phi")
    return lax.ppermute(value, "phi", [(s, (s + steps) % count) for s in range(count)])


def permute_sibling(value):
    count = lax.axis_size("phi")
    return lax.ppermute(value, "phi", [(s, s ^ 1) for s in range(count)])


def permute_cross(value):
    count = lax.axis_size("phi")
    return lax.ppermute(
        value, "phi", [(s, (s + (1 if s % 2 else -1)) % count) for s in range(count)]
    )


def window_pieces(latents, is_even):
    below = permute_far(latents, 2)
    above = permute_far(latents, -2)
    sibling = permute_sibling(latents)
    cross = permute_sibling(jnp.where(is_even, above, below))
    return below, latents, above, sibling, cross


def return_pieces(below, above, sibling, cross, is_even):
    cross_in = permute_sibling(cross).astype(F32)
    sibling_in = permute_sibling(sibling)
    zero = jnp.zeros((), F32)
    above_out = (above + jnp.where(is_even, cross_in, zero)).astype(BF16)
    below_out = (below + jnp.where(is_even, zero, cross_in)).astype(BF16)
    from_below = permute_far(above_out, 2)
    from_above = permute_far(below_out, -2)
    return from_below, from_above, sibling_in


def aggregate_group(index_ref, tiles_ref, window_ref, step, group, slots, rows, zero_ok=None):
    results = []
    for g in range(group):
        tile = jnp.concatenate([tiles_ref[g, s] for s in range(slots)], axis=1)
        source = jnp.concatenate(
            [
                window_ref[
                    pl.ds(
                        pl.multiple_of(index_ref[(step * group + g) * slots + s] * rows, rows),
                        rows,
                    ),
                    :,
                ]
                for s in range(slots)
            ],
            axis=0,
        )
        results.append(dot(tile, source, 1, 0).astype(BF16))
    return jnp.concatenate(results, axis=0)


def node_update(own, aggregated, w_self, w_agg, w_out):
    activation = dot(own, w_self, 1, 0) + dot(aggregated, w_agg, 1, 0)
    hidden = jnp.maximum(activation, 0.0).astype(BF16)
    updated = (own.astype(F32) + dot(hidden, w_out, 1, 0)).astype(BF16)
    return hidden, updated


def first_forward(
    group,
    index_ref,
    tiles_ref,
    feats_ref,
    wcat_ref,
    w_self_ref,
    w_agg_ref,
    w_out_ref,
    before_ref,
    agg_ref,
    hidden_ref,
    updated_ref,
    window_ref,
):
    step = pl.program_id(0)
    slots, rows = tiles_ref.shape[1], tiles_ref.shape[2]
    span = group * rows
    total = feats_ref.shape[1]

    @pl.when(step == 0)
    def _():
        def encode(i, carry):
            at = pl.multiple_of(i * 512, 512)
            encoded = dot(feats_ref[:, pl.ds(at, 512)], wcat_ref[...], 0, 0)
            window_ref[pl.ds(at, 512), :] = jnp.tanh(encoded).astype(BF16)
            return carry

        lax.fori_loop(0, total // 512, encode, 0)
        window_ref[pl.ds(total, rows), :] = jnp.zeros((rows, window_ref.shape[1]), BF16)

    aggregated = aggregate_group(index_ref, tiles_ref, window_ref, step, group, slots, rows)
    own = window_ref[pl.ds(pl.multiple_of(total // 5 + step * span, span), span), :]
    hidden, updated = node_update(own, aggregated, w_self_ref[...], w_agg_ref[...], w_out_ref[...])
    before_ref[...] = own
    agg_ref[...] = aggregated
    hidden_ref[...] = hidden
    updated_ref[...] = updated


def later_forward(
    group,
    index_ref,
    tiles_ref,
    below_ref,
    own_ref,
    above_ref,
    sibling_ref,
    cross_ref,
    w_self_ref,
    w_agg_ref,
    w_out_ref,
    agg_ref,
    hidden_ref,
    updated_ref,
    window_ref,
    sems,
):
    step = pl.program_id(0)
    slots, rows = tiles_ref.shape[1], tiles_ref.shape[2]
    span = group * rows
    hits = own_ref.shape[0]

    @pl.when(step == 0)
    def _():
        copies = [
            pltpu.make_async_copy(piece, window_ref.at[pl.ds(k * hits, hits)], sems.at[k])
            for k, piece in enumerate((below_ref, own_ref, above_ref, sibling_ref, cross_ref))
        ]
        for copy in copies:
            copy.start()
        window_ref[pl.ds(5 * hits, rows), :] = jnp.zeros((rows, window_ref.shape[1]), BF16)
        for copy in copies:
            copy.wait()

    aggregated = aggregate_group(index_ref, tiles_ref, window_ref, step, group, slots, rows)
    own = window_ref[pl.ds(pl.multiple_of(hits + step * span, span), span), :]
    hidden, updated = node_update(own, aggregated, w_self_ref[...], w_agg_ref[...], w_out_ref[...])
    agg_ref[...] = aggregated
    hidden_ref[...] = hidden
    updated_ref[...] = updated


def contrast_kernel(
    inv_root,
    anchor_ref,
    positive_ref,
    negative_ref,
    below_ref,
    own_ref,
    above_ref,
    sibling_ref,
    cross_ref,
    loss_ref,
    gbelow_ref,
    gown_ref,
    gabove_ref,
    gsibling_ref,
    gcross_ref,
    window_ref,
    grad_pos_ref,
    grad_neg_ref,
    grad_anchor_ref,
    a_ref,
    p_ref,
    n_ref,
):
    hits = own_ref.shape[0]
    count = a_ref.shape[0]
    width = own_ref.shape[1]
    for k, piece in enumerate((below_ref, own_ref, above_ref, sibling_ref, cross_ref)):

        def widen(i, carry, k=k, piece=piece):
            at = pl.multiple_of(i * 256, 256)
            window_ref[pl.ds(k * hits + at, 256), :] = piece[pl.ds(at, 256), :].astype(F32)
            zeros = jnp.zeros((256, width), F32)
            grad_pos_ref[pl.ds(k * hits + at, 256), :] = zeros
            grad_neg_ref[pl.ds(k * hits + at, 256), :] = zeros
            if k == 0:
                grad_anchor_ref[pl.ds(at, 256), :] = zeros
            return carry

        lax.fori_loop(0, hits // 256, widen, 0)

    def fetch(i, carry):
        at = pl.multiple_of(i * 8, 8)
        for index_ref, offset, target in (
            (anchor_ref, hits, a_ref),
            (positive_ref, 0, p_ref),
            (negative_ref, 0, n_ref),
        ):
            target[pl.ds(at, 8), :] = jnp.concatenate(
                [window_ref[pl.ds(index_ref[i * 8 + u] + offset, 1), :] for u in range(8)], axis=0
            )
        return carry

    lax.fori_loop(0, count // 8, fetch, 0)

    def score(i, total):
        at = pl.multiple_of(i * 128, 128)
        anchor = a_ref[pl.ds(at, 128), :]
        positive = p_ref[pl.ds(at, 128), :]
        negative = n_ref[pl.ds(at, 128), :]
        gap = (
            jnp.sum(anchor * negative, axis=1, keepdims=True)
            - jnp.sum(anchor * positive, axis=1, keepdims=True)
        ) * inv_root
        soft = jnp.maximum(gap, 0.0) + jnp.log1p(jnp.exp(-jnp.abs(gap)))
        coef = jax.nn.sigmoid(gap) * (inv_root / loss_divisor)
        p_ref[pl.ds(at, 128), :] = coef * (negative - positive)
        a_ref[pl.ds(at, 128), :] = coef * anchor
        return total + jnp.sum(soft, axis=0, keepdims=True)

    total = lax.fori_loop(0, count // 128, score, jnp.zeros((1, 1), F32))
    loss_ref[...] = jnp.broadcast_to(total, loss_ref.shape)

    def spread(i, carry):
        for u in range(8):
            t = i * 8 + u
            moved = a_ref[pl.ds(t, 1), :]
            here = pl.ds(anchor_ref[t], 1)
            grad_anchor_ref[here, :] = grad_anchor_ref[here, :] + p_ref[pl.ds(t, 1), :]
            there = pl.ds(positive_ref[t], 1)
            grad_pos_ref[there, :] = grad_pos_ref[there, :] - moved
            away = pl.ds(negative_ref[t], 1)
            grad_neg_ref[away, :] = grad_neg_ref[away, :] + moved
        return carry

    lax.fori_loop(0, count // 8, spread, 0)

    for k, target in enumerate((gbelow_ref, gown_ref, gabove_ref, gsibling_ref, gcross_ref)):

        def merge(i, carry, k=k, target=target):
            at = pl.multiple_of(i * 256, 256)
            value = grad_pos_ref[pl.ds(k * hits + at, 256), :] + grad_neg_ref[
                pl.ds(k * hits + at, 256), :
            ]
            if k == 1:
                value = value + grad_anchor_ref[pl.ds(at, 256), :]
            target[pl.ds(at, 256), :] = value.astype(target.dtype)
            return carry

        lax.fori_loop(0, hits // 256, merge, 0)


def node_backward(
    gradient, hidden_ref, before_ref, agg_ref, w_out, gout_ref, gself_ref, gagg_ref, step
):
    upstream = gradient.astype(BF16)
    hidden = hidden_ref[...]
    hidden_grad = dot(upstream, w_out, 1, 1)
    act_grad = jnp.where(hidden.astype(F32) > 0, hidden_grad, 0.0).astype(BF16)

    @pl.when(step == 0)
    def _():
        gout_ref[...] = jnp.zeros(gout_ref.shape, F32)
        gself_ref[...] = jnp.zeros(gself_ref.shape, F32)
        gagg_ref[...] = jnp.zeros(gagg_ref.shape, F32)

    gout_ref[...] += dot(hidden, upstream, 0, 0)
    gself_ref[...] += dot(before_ref[...], act_grad, 0, 0)
    gagg_ref[...] += dot(agg_ref[...], act_grad, 0, 0)
    return act_grad


def spread_group(index_ref, tiles_ref, adj_ref, agg_grad_t, step, group, slots, rows):
    for g in range(group):
        tile = jnp.concatenate([tiles_ref[g, s] for s in range(slots)], axis=1)
        contrib = dot(agg_grad_t[:, g * rows : (g + 1) * rows], tile, 1, 0)
        for s in range(slots):
            at = index_ref[(step * group + g) * slots + s]
            adj_ref[at] = adj_ref[at] + contrib[:, s * rows : (s + 1) * rows]


def clear_blocks(adj_ref):
    def clear(i, carry):
        adj_ref[i] = jnp.zeros(adj_ref.shape[1:], F32)
        return carry

    lax.fori_loop(0, adj_ref.shape[0], clear, 0)


def last_backward(
    group,
    steps,
    index_ref,
    tiles_ref,
    own_ref,
    down_ref,
    up_ref,
    sib_ref,
    hidden_ref,
    before_ref,
    agg_ref,
    w_self_ref,
    w_agg_ref,
    w_out_ref,
    gout_ref,
    gself_ref,
    gagg_ref,
    direct_ref,
    obelow_ref,
    oown_ref,
    oabove_ref,
    osibling_ref,
    ocross_ref,
    adj_ref,
):
    step = pl.program_id(0)
    slots, rows = tiles_ref.shape[1], tiles_ref.shape[2]

    @pl.when(step == 0)
    def _():
        clear_blocks(adj_ref)

    gradient = own_ref[...] + (
        (down_ref[...].astype(F32) + up_ref[...].astype(F32)) + sib_ref[...].astype(F32)
    )
    act_grad = node_backward(
        gradient, hidden_ref, before_ref, agg_ref, w_out_ref[...], gout_ref, gself_ref, gagg_ref, step
    )
    direct_ref[...] = gradient + dot(act_grad, w_self_ref[...], 1, 1)
    agg_grad_t = dot(w_agg_ref[...], act_grad, 1, 1).astype(BF16)
    spread_group(index_ref, tiles_ref, adj_ref, agg_grad_t, step, group, slots, rows)

    @pl.when(step == steps - 1)
    def _():
        blocks = oown_ref.shape[0]
        for k, target in enumerate((obelow_ref, oown_ref, oabove_ref, osibling_ref, ocross_ref)):

            def store(i, carry, k=k, target=target):
                target[i] = adj_ref[k * blocks + i].astype(target.dtype)
                return carry

            lax.fori_loop(0, blocks, store, 0)


def first_backward(
    group,
    steps,
    index_ref,
    tiles_ref,
    direct_ref,
    own_ref,
    down_ref,
    up_ref,
    sib_ref,
    hidden_ref,
    before_ref,
    agg_ref,
    w_self_ref,
    w_agg_ref,
    w_out_ref,
    feats_ref,
    wcat_ref,
    wcat_t_ref,
    gout_ref,
    gself_ref,
    gagg_ref,
    genc_ref,
    adj_ref,
):
    step = pl.program_id(0)
    slots, rows = tiles_ref.shape[1], tiles_ref.shape[2]
    span = group * rows
    total = feats_ref.shape[1]

    @pl.when(step == 0)
    def _():
        clear_blocks(adj_ref)
        genc_ref[...] = jnp.zeros(genc_ref.shape, F32)

    pieces = []
    for g in range(group):
        returned = own_ref[g] + (
            (down_ref[g].astype(F32) + up_ref[g].astype(F32)) + sib_ref[g].astype(F32)
        )
        pieces.append(returned.T)
    gradient = direct_ref[...] + jnp.concatenate(pieces, axis=0)
    act_grad = node_backward(
        gradient, hidden_ref, before_ref, agg_ref, w_out_ref[...], gout_ref, gself_ref, gagg_ref, step
    )
    direct = gradient + dot(act_grad, w_self_ref[...], 1, 1)
    here = feats_ref[:, pl.ds(pl.multiple_of(total // 5 + step * span, span), span)]
    squashed = jnp.tanh(dot(here, wcat_ref[...], 0, 0))
    genc_ref[...] += dot(here, (direct * (1.0 - squashed * squashed)).astype(BF16), 1, 0)
    agg_grad_t = dot(w_agg_ref[...], act_grad, 1, 1).astype(BF16)
    spread_group(index_ref, tiles_ref, adj_ref, agg_grad_t, step, group, slots, rows)

    @pl.when(step == steps - 1)
    def _():
        per = 4

        def encode(i, carry):
            at = pl.multiple_of(i * (per * rows), per * rows)
            feats = feats_ref[:, pl.ds(at, per * rows)]
            squashed_t = jnp.tanh(dot(wcat_t_ref[...], feats, 1, 0))
            grad_t = jnp.concatenate([adj_ref[i * per + u] for u in range(per)], axis=1)
            grad_t = (grad_t * (1.0 - squashed_t * squashed_t)).astype(BF16)
            return carry + dot(feats, grad_t, 1, 1)

        genc_ref[...] += lax.fori_loop(
            0, total // (per * rows), encode, jnp.zeros(genc_ref.shape, F32)
        )


def body(
    hit_feats,
    layer_ids,
    edge_tiles,
    src_blocks,
    live_slots,
    anchor_hits,
    positive_hits,
    negative_hits,
    w_enc,
    layer_table,
    w_self,
    w_agg,
    w_out,
):
    blocks, slots, rows, _ = edge_tiles.shape
    width = w_enc.shape[1]
    features = hit_feats.shape[0]
    kinds = layer_table.shape[0]
    hits = blocks * rows
    layer_total = w_self.shape[0]
    triplets = anchor_hits.shape[0]
    group = 4
    steps = blocks // group
    span = group * rows
    is_even = lax.rem(lax.axis_index("phi"), 2) == 0

    def place(part):
        odd = jnp.where(is_even, 4, 3)
        near = jnp.where(is_even, 3, 4)
        return jnp.where(
            part == 0,
            0,
            jnp.where(part == 2, 1, jnp.where(part == 4, 2, jnp.where(part == 1, odd, near))),
        )

    live = jnp.arange(slots, dtype=jnp.int32)[None, :] < live_slots[:, None]
    index = jnp.where(
        live, place(src_blocks // blocks) * blocks + src_blocks % blocks, 5 * blocks
    ).reshape(blocks * slots)
    positive = place(positive_hits // hits) * hits + positive_hits % hits
    negative = place(negative_hits // hits) * hits + negative_hits % hits

    pad = -(features + 1) % 16
    packed = jnp.concatenate(
        [hit_feats, layer_ids.astype(BF16)[None, :], jnp.zeros((pad, hits), BF16)], axis=0
    )
    packed = jnp.concatenate(
        [
            permute_far(packed, 2),
            packed,
            permute_far(packed, -2),
            permute_sibling(packed),
            permute_cross(packed),
        ],
        axis=1,
    )
    feature_pad = -features % 16
    onehot = (
        jnp.arange(kinds, dtype=jnp.int32)[:, None].astype(BF16) == packed[features][None, :]
    ).astype(BF16)
    feats = jnp.concatenate(
        [packed[:features], jnp.zeros((feature_pad, 5 * hits), BF16), onehot], axis=0
    )
    wcat = jnp.concatenate([w_enc, jnp.zeros((feature_pad, width), BF16), layer_table], axis=0)
    depth = wcat.shape[0]

    tile_spec = pl.BlockSpec((group, slots, rows, rows), lambda i, *_: (i, 0, 0, 0))
    row_spec = pl.BlockSpec((span, width), lambda i, *_: (i, 0))
    block_spec = pl.BlockSpec((group, width, rows), lambda i, *_: (i, 0, 0))
    weight_spec = full((width, width))
    any_spec = pl.BlockSpec(memory_space=pl.ANY)
    row_shape = jax.ShapeDtypeStruct((hits, width), BF16)
    weight_shape = jax.ShapeDtypeStruct((width, width), F32)

    before0, agg0, hidden0, latents = pl.pallas_call(
        functools.partial(first_forward, group),
        grid_spec=pltpu.PrefetchScalarGridSpec(
            num_scalar_prefetch=1,
            grid=(steps,),
            in_specs=[tile_spec, full((depth, 5 * hits)), full((depth, width))] + [weight_spec] * 3,
            out_specs=[row_spec] * 4,
            scratch_shapes=[pltpu.VMEM((5 * hits + rows, width), BF16)],
        ),
        out_shape=[row_shape] * 4,
        compiler_params=params(),
        name="first_forward",
    )(index, edge_tiles, feats, wcat, w_self[0], w_agg[0], w_out[0])
    stored = [(before0, agg0, hidden0)]
    for layer in range(1, layer_total):
        pieces = window_pieces(latents, is_even)
        aggregated, hidden, updated = pl.pallas_call(
            functools.partial(later_forward, group),
            grid_spec=pltpu.PrefetchScalarGridSpec(
                num_scalar_prefetch=1,
                grid=(steps,),
                in_specs=[tile_spec] + [any_spec] * 5 + [weight_spec] * 3,
                out_specs=[row_spec] * 3,
                scratch_shapes=[
                    pltpu.VMEM((5 * hits + rows, width), BF16),
                    pltpu.SemaphoreType.DMA((5,)),
                ],
            ),
            out_shape=[row_shape] * 3,
            compiler_params=params(),
            name="later_forward",
        )(index, edge_tiles, *pieces, w_self[layer], w_agg[layer], w_out[layer])
        stored.append((latents, aggregated, hidden))
        latents = updated

    pieces = window_pieces(latents, is_even)
    wide_shape = jax.ShapeDtypeStruct((hits, width), F32)
    whole = full((hits, width))
    loss_part, gbelow, gown, gabove, gsibling, gcross = pl.pallas_call(
        functools.partial(contrast_kernel, 1.0 / math.sqrt(width)),
        grid_spec=pltpu.PrefetchScalarGridSpec(
            num_scalar_prefetch=3,
            grid=(1,),
            in_specs=[pl.BlockSpec((hits, width), lambda *_: (0, 0), pipeline_mode=pl.Buffered(1))] * 5,
            out_specs=[full((8, width))]
            + [pl.BlockSpec((hits, width), lambda *_: (0, 0), pipeline_mode=pl.Buffered(1))] * 5,
            scratch_shapes=[pltpu.VMEM((5 * hits, width), F32)] * 3
            + [pltpu.VMEM((hits, width), F32)]
            + [pltpu.VMEM((triplets, width), F32)] * 3,
        ),
        out_shape=[jax.ShapeDtypeStruct((8, width), F32)]
        + [wide_shape] * 3
        + [row_shape] * 2,
        compiler_params=params(),
        name="contrast",
    )(anchor_hits, positive, negative, *pieces)
    down, up, sib = return_pieces(gbelow, gabove, gsibling, gcross, is_even)

    t_shape = jax.ShapeDtypeStruct((blocks, width, rows), F32)
    t_half = jax.ShapeDtypeStruct((blocks, width, rows), BF16)
    t_full = pl.BlockSpec(
        (blocks, width, rows), lambda *_: (0, 0, 0), pipeline_mode=pl.Buffered(1)
    )
    adj_shape = pltpu.VMEM((5 * blocks + 1, width, rows), F32)
    own = gown
    before, aggregated, hidden = stored[1]
    gout1, gself1, gagg1, direct, obelow, own, oabove, osibling, ocross = pl.pallas_call(
        functools.partial(last_backward, group, steps),
        grid_spec=pltpu.PrefetchScalarGridSpec(
            num_scalar_prefetch=1,
            grid=(steps,),
            in_specs=[tile_spec] + [row_spec] * 7 + [weight_spec] * 3,
            out_specs=[weight_spec] * 3 + [row_spec] + [t_full] * 5,
            scratch_shapes=[adj_shape],
        ),
        out_shape=[weight_shape] * 3 + [wide_shape] + [t_shape] * 3 + [t_half] * 2,
        compiler_params=params(),
        name="last_backward",
    )(
        index, edge_tiles, own, down, up, sib, hidden, before, aggregated,
        w_self[1], w_agg[1], w_out[1],
    )
    early = lax.psum(jnp.concatenate([gout1, gself1, gagg1, loss_part], axis=0), "phi")
    down, up, sib = return_pieces(obelow, oabove, osibling, ocross, is_even)
    before, aggregated, hidden = stored[0]
    gout0, gself0, gagg0, genc = pl.pallas_call(
        functools.partial(first_backward, group, steps),
        grid_spec=pltpu.PrefetchScalarGridSpec(
            num_scalar_prefetch=1,
            grid=(steps,),
            in_specs=[tile_spec, row_spec]
            + [block_spec] * 4
            + [row_spec] * 3
            + [weight_spec] * 3
            + [full((depth, 5 * hits)), full((depth, width)), full((width, depth))],
            out_specs=[weight_spec] * 3 + [full((depth, width))],
            scratch_shapes=[adj_shape],
        ),
        out_shape=[weight_shape] * 3 + [jax.ShapeDtypeStruct((depth, width), F32)],
        compiler_params=params(),
        name="first_backward",
    )(
        index, edge_tiles, direct, own, down, up, sib, hidden, before, aggregated,
        w_self[0], w_agg[0], w_out[0], feats, wcat, wcat.T,
    )
    late = lax.psum(jnp.concatenate([gout0, gself0, gagg0, genc], axis=0), "phi")

    triplet_total = triplets * lax.axis_size("phi")
    loss = (early[3 * width, 0] / triplet_total).reshape(1)
    base = 3 * width
    grad_enc = late[base : base + features]
    grad_table = late[base + depth - kinds : base + depth]

    def pair(k):
        return jnp.stack([late[k * width : (k + 1) * width], early[k * width : (k + 1) * width]])

    return (loss, grad_enc, grad_table, pair(1), pair(2), pair(0))


def solution(mesh):
    both = ("event", "phi")
    in_specs = (
        P(None, both),
        P(both),
        P(both, None, None, None),
        P(both, None),
        P(both),
        P(both),
        P(both),
        P(both),
        P(),
        P(),
        P(),
        P(),
        P(),
    )
    out_specs = (
        P("event"),
        P("event", None),
        P("event", None),
        P("event", None, None),
        P("event", None, None),
        P("event", None, None),
    )
    return jax.shard_map(body, mesh=mesh, in_specs=in_specs, out_specs=out_specs, check_vma=False)
```

```python
import functools
import math

import jax
import jax.numpy as jnp
from jax import lax
from jax.experimental import pallas as pl
from jax.experimental.pallas import tpu as pltpu
from jax.sharding import PartitionSpec as P

loss_divisor = 64.0
F32 = jnp.float32
BF16 = jnp.bfloat16
VMEM_BYTES = 60 * 1024 * 1024


def dot(left, right, left_dim, right_dim):
    return lax.dot_general(
        left, right, (((left_dim,), (right_dim,)), ((), ())), preferred_element_type=F32
    )


def full(shape):
    return pl.BlockSpec(shape, lambda *_: (0,) * len(shape))


def params():
    return pltpu.CompilerParams(
        dimension_semantics=("arbitrary",), vmem_limit_bytes=VMEM_BYTES
    )


CHUNKS = 8


def permute(value, target_of):
    count = lax.axis_size("phi")
    return lax.ppermute(value, "phi", [(s, target_of(s) % count) for s in range(count)])


def direct_target(s):
    return s ^ 2


def relayed_target(s):
    return s + 2 if (s // 2) % 2 else s - 2


def sibling_target(s):
    return s ^ 1


def cross_target(s):
    return s + 1 if s % 2 else s - 1


def peers():
    count = lax.axis_size("phi")
    me = lax.axis_index("phi")
    odd_pair = (me // 2) % 2
    odd_core = me % 2
    direct = me + 2 - 4 * odd_pair
    sibling = me + 1 - 2 * odd_core
    stride = 4 - 8 * odd_pair
    onward = (me + stride + count) % count
    source = (me - stride + count) % count
    return direct, sibling, onward, source, odd_pair == odd_core


def remote(src, dst, send, recv, target):
    return pltpu.make_async_remote_copy(
        src_ref=src,
        dst_ref=dst,
        send_sem=send,
        recv_sem=recv,
        device_id={"phi": target},
        device_id_type=pl.DeviceIdType.MESH,
    )


def greet(targets):
    barrier = pltpu.get_barrier_semaphore()
    for target in targets:
        pl.semaphore_signal(
            barrier, inc=1, device_id={"phi": target}, device_id_type=pl.DeviceIdType.MESH
        )
    pl.semaphore_wait(barrier, len(targets))


def exchange_kernel(own, direct_out, relay_out, sib_out, cross_out, *sems):
    ys, yr, zs, zr, cs, cr, ss, sr = sems
    direct, sibling, onward, source, direct_crosses = peers()
    size = own.shape[0] // CHUNKS
    greet((direct, sibling, source))

    def part(ref, i):
        return ref.at[pl.ds(i * size, size)]

    first = [
        remote(part(own, i), part(direct_out, i), ys.at[i], yr.at[i], direct) for i in range(CHUNKS)
    ]
    second = [
        remote(part(direct_out, i), part(relay_out, i), zs.at[i], zr.at[i], onward)
        for i in range(CHUNKS)
    ]
    cross_a = [
        remote(part(direct_out, i), part(cross_out, i), cs.at[i], cr.at[i], sibling)
        for i in range(CHUNKS)
    ]
    cross_b = [
        remote(part(relay_out, i), part(cross_out, i), cs.at[i], cr.at[i], sibling)
        for i in range(CHUNKS)
    ]
    near = remote(own, sib_out, ss.at[0], sr.at[0], sibling)
    for copy in first:
        copy.start()
    near.start()
    for i in range(CHUNKS):
        first[i].wait_recv()
        second[i].start()

        @pl.when(direct_crosses)
        def _():
            cross_a[i].start()

    for i in range(CHUNKS):
        second[i].wait_recv()

        @pl.when(jnp.logical_not(direct_crosses))
        def _():
            cross_b[i].start()

    near.wait()
    for i in range(CHUNKS):
        first[i].wait_send()
        second[i].wait_send()
        cross_a[i].wait()


def window_pieces(latents):
    hits, width = latents.shape
    any_spec = pl.BlockSpec(memory_space=pl.ANY)
    direct, relayed, sibling, cross = pl.pallas_call(
        exchange_kernel,
        in_specs=[any_spec],
        out_specs=[any_spec] * 4,
        out_shape=[jax.ShapeDtypeStruct((hits, width), BF16)] * 4,
        scratch_shapes=[pltpu.SemaphoreType.DMA((CHUNKS,))] * 6 + [pltpu.SemaphoreType.DMA((1,))] * 2,
        compiler_params=pltpu.CompilerParams(collective_id=1, has_side_effects=True),
        name="exchange",
    )(latents)
    return direct, latents, relayed, sibling, cross


def return_kernel(
    direct_ref,
    relay_ref,
    sib_ref,
    cross_ref,
    total_out,
    sib_out,
    cross_in,
    relay_send,
    relay_in,
    direct_send,
    *sems,
):
    ys, yr, zs, zr, cs, cr, ss, sr = sems
    direct, sibling, onward, source, to_direct = peers()
    size = direct_ref.shape[0] // CHUNKS
    greet((direct, sibling, onward))

    def rows(i):
        return pl.ds(i * size, size)

    crosses = [
        remote(cross_ref.at[rows(i)], cross_in.at[rows(i)], cs.at[i], cr.at[i], sibling)
        for i in range(CHUNKS)
    ]
    first = [
        remote(relay_send.at[rows(i)], relay_in.at[rows(i)], zs.at[i], zr.at[i], source)
        for i in range(CHUNKS)
    ]
    second = [
        remote(direct_send.at[rows(i)], total_out.at[rows(i)], ys.at[i], yr.at[i], direct)
        for i in range(CHUNKS)
    ]
    near = remote(sib_ref, sib_out, ss.at[0], sr.at[0], sibling)
    for copy in crosses:
        copy.start()
    near.start()
    for i in range(CHUNKS):
        crosses[i].wait_recv()
        extra = jnp.where(to_direct, 0.0, cross_in[rows(i), :].astype(F32))
        relay_send[rows(i), :] = (relay_ref[rows(i), :] + extra).astype(BF16)
        first[i].start()
    for i in range(CHUNKS):
        first[i].wait_recv()
        extra = jnp.where(to_direct, cross_in[rows(i), :].astype(F32), 0.0)
        direct_send[rows(i), :] = (
            direct_ref[rows(i), :] + extra + relay_in[rows(i), :].astype(F32)
        ).astype(BF16)
        second[i].start()
    near.wait()
    for i in range(CHUNKS):
        crosses[i].wait_send()
        first[i].wait_send()
        second[i].wait()


def return_pieces(direct, relayed, sibling, cross):
    shape = sibling.shape
    hits, width = math.prod(shape[:-1]), shape[-1]
    vmem = pl.BlockSpec(memory_space=pltpu.VMEM)
    half = jax.ShapeDtypeStruct((hits, width), BF16)
    total, sib = pl.pallas_call(
        return_kernel,
        in_specs=[vmem] * 4,
        out_specs=[vmem] * 2,
        out_shape=[half] * 2,
        scratch_shapes=[pltpu.VMEM((hits, width), BF16)] * 4
        + [pltpu.SemaphoreType.DMA((CHUNKS,))] * 6
        + [pltpu.SemaphoreType.DMA((1,))] * 2,
        compiler_params=pltpu.CompilerParams(
            collective_id=2, has_side_effects=True, vmem_limit_bytes=VMEM_BYTES
        ),
        name="give_back",
    )(*[piece.reshape(hits, width) for piece in (direct, relayed, sibling, cross)])
    return total.reshape(shape), sib.reshape(shape)


def sum_kernel(
    pairs, x_ref, out_ref, half_in, acc_ref, slots_in, all_ref, s0, r0, s1, r1, s2, r2, s3, r3
):
    me = lax.axis_index("phi")
    pair, core = me // 2, me % 2
    sibling = me + 1 - 2 * core
    half = x_ref.shape[0] // 2
    chunk = half // pairs
    others = [((pair + d) % pairs) * 2 + core for d in range(1, pairs)]
    greet([sibling] + others)

    def span(start, size):
        return pl.ds(pl.multiple_of(start, 8), size)

    swap = remote(x_ref.at[span((1 - core) * half, half)], half_in, s0.at[0], r0.at[0], sibling)
    swap.start()
    swap.wait()
    acc_ref[...] = x_ref[span(core * half, half), :] + half_in[...]
    scatter = [
        remote(
            acc_ref.at[span(((pair + d) % pairs) * chunk, chunk)],
            slots_in.at[d - 1],
            s1.at[d - 1],
            r1.at[d - 1],
            others[d - 1],
        )
        for d in range(1, pairs)
    ]
    for copy in scatter:
        copy.start()
    total = acc_ref[span(pair * chunk, chunk), :]
    for d in range(1, pairs):
        scatter[d - 1].wait_recv()
        total = total + slots_in[d - 1]
    mine = span(core * half + pair * chunk, chunk)
    all_ref[mine, :] = total
    gather = [
        remote(all_ref.at[mine], all_ref.at[mine], s2.at[d - 1], r2.at[d - 1], others[d - 1])
        for d in range(1, pairs)
    ]
    for copy in gather:
        copy.start()
    for copy in gather:
        copy.wait()
    for copy in scatter:
        copy.wait_send()
    whole = span(core * half, half)
    last = remote(all_ref.at[whole], all_ref.at[whole], s3.at[0], r3.at[0], sibling)
    last.start()
    last.wait()
    out_ref[...] = all_ref[...]


def sum_all(value):
    pairs = lax.axis_size("phi") // 2
    rows, width = value.shape
    chunk = -(-rows // (16 * pairs)) * 8
    total = 2 * pairs * chunk
    value = jnp.concatenate([value, jnp.zeros((total - rows, width), F32)], axis=0)
    vmem = pl.BlockSpec(memory_space=pltpu.VMEM)
    one = pltpu.SemaphoreType.DMA((1,))
    many = pltpu.SemaphoreType.DMA((pairs - 1,))
    return pl.pallas_call(
        functools.partial(sum_kernel, pairs),
        in_specs=[vmem],
        out_specs=vmem,
        out_shape=jax.ShapeDtypeStruct((total, width), F32),
        scratch_shapes=[
            pltpu.VMEM((total // 2, width), F32),
            pltpu.VMEM((total // 2, width), F32),
            pltpu.VMEM((pairs - 1, chunk, width), F32),
            pltpu.VMEM((total, width), F32),
            one, one, many, many, many, many, one, one,
        ],
        compiler_params=pltpu.CompilerParams(
            collective_id=3, has_side_effects=True, vmem_limit_bytes=VMEM_BYTES
        ),
        name="sum_all",
    )(value)


def aggregate_group(index_ref, tiles_ref, window_ref, step, group, slots, rows):
    results = []
    for g in range(group):
        tile = jnp.concatenate([tiles_ref[g, s] for s in range(slots)], axis=1)
        source = jnp.concatenate(
            [
                window_ref[
                    pl.ds(
                        pl.multiple_of(index_ref[(step * group + g) * slots + s] * rows, rows),
                        rows,
                    ),
                    :,
                ]
                for s in range(slots)
            ],
            axis=0,
        )
        results.append(dot(tile, source, 1, 0).astype(BF16))
    return jnp.concatenate(results, axis=0)


def node_update(own, aggregated, w_self, w_agg, w_out):
    activation = dot(own, w_self, 1, 0) + dot(aggregated, w_agg, 1, 0)
    hidden = jnp.maximum(activation, 0.0).astype(BF16)
    updated = (own.astype(F32) + dot(hidden, w_out, 1, 0)).astype(BF16)
    return hidden, updated


def first_forward(
    group,
    index_ref,
    tiles_ref,
    feats_ref,
    wcat_ref,
    w_self_ref,
    w_agg_ref,
    w_out_ref,
    before_ref,
    agg_ref,
    hidden_ref,
    updated_ref,
    window_ref,
):
    step = pl.program_id(0)
    slots, rows = tiles_ref.shape[1], tiles_ref.shape[2]
    span = group * rows
    total = feats_ref.shape[1]

    @pl.when(step == 0)
    def _():
        def encode(i, carry):
            at = pl.multiple_of(i * 512, 512)
            encoded = dot(feats_ref[:, pl.ds(at, 512)], wcat_ref[...], 0, 0)
            window_ref[pl.ds(at, 512), :] = jnp.tanh(encoded).astype(BF16)
            return carry

        lax.fori_loop(0, total // 512, encode, 0)
        window_ref[pl.ds(total, rows), :] = jnp.zeros((rows, window_ref.shape[1]), BF16)

    aggregated = aggregate_group(index_ref, tiles_ref, window_ref, step, group, slots, rows)
    own = window_ref[pl.ds(pl.multiple_of(total // 5 + step * span, span), span), :]
    hidden, updated = node_update(own, aggregated, w_self_ref[...], w_agg_ref[...], w_out_ref[...])
    before_ref[...] = own
    agg_ref[...] = aggregated
    hidden_ref[...] = hidden
    updated_ref[...] = updated


def later_forward(
    group,
    index_ref,
    tiles_ref,
    below_ref,
    own_ref,
    above_ref,
    sibling_ref,
    cross_ref,
    w_self_ref,
    w_agg_ref,
    w_out_ref,
    agg_ref,
    hidden_ref,
    updated_ref,
    window_ref,
    sems,
):
    step = pl.program_id(0)
    slots, rows = tiles_ref.shape[1], tiles_ref.shape[2]
    span = group * rows
    hits = own_ref.shape[0]

    @pl.when(step == 0)
    def _():
        copies = [
            pltpu.make_async_copy(piece, window_ref.at[pl.ds(k * hits, hits)], sems.at[k])
            for k, piece in enumerate((below_ref, own_ref, above_ref, sibling_ref, cross_ref))
        ]
        for copy in copies:
            copy.start()
        window_ref[pl.ds(5 * hits, rows), :] = jnp.zeros((rows, window_ref.shape[1]), BF16)
        for copy in copies:
            copy.wait()

    aggregated = aggregate_group(index_ref, tiles_ref, window_ref, step, group, slots, rows)
    own = window_ref[pl.ds(pl.multiple_of(hits + step * span, span), span), :]
    hidden, updated = node_update(own, aggregated, w_self_ref[...], w_agg_ref[...], w_out_ref[...])
    agg_ref[...] = aggregated
    hidden_ref[...] = hidden
    updated_ref[...] = updated


def contrast_kernel(
    inv_root,
    anchor_ref,
    positive_ref,
    negative_ref,
    below_ref,
    own_ref,
    above_ref,
    sibling_ref,
    cross_ref,
    loss_ref,
    gbelow_ref,
    gown_ref,
    gabove_ref,
    gsibling_ref,
    gcross_ref,
    window_ref,
    grad_pos_ref,
    grad_neg_ref,
    grad_anchor_ref,
    a_ref,
    p_ref,
    n_ref,
):
    hits = own_ref.shape[0]
    count = a_ref.shape[0]
    width = own_ref.shape[1]
    for k, piece in enumerate((below_ref, own_ref, above_ref, sibling_ref, cross_ref)):

        def widen(i, carry, k=k, piece=piece):
            at = pl.multiple_of(i * 256, 256)
            window_ref[pl.ds(k * hits + at, 256), :] = piece[pl.ds(at, 256), :].astype(F32)
            zeros = jnp.zeros((256, width), F32)
            grad_pos_ref[pl.ds(k * hits + at, 256), :] = zeros
            grad_neg_ref[pl.ds(k * hits + at, 256), :] = zeros
            if k == 0:
                grad_anchor_ref[pl.ds(at, 256), :] = zeros
            return carry

        lax.fori_loop(0, hits // 256, widen, 0)

    def fetch(i, carry):
        at = pl.multiple_of(i * 8, 8)
        for index_ref, offset, target in (
            (anchor_ref, hits, a_ref),
            (positive_ref, 0, p_ref),
            (negative_ref, 0, n_ref),
        ):
            target[pl.ds(at, 8), :] = jnp.concatenate(
                [window_ref[pl.ds(index_ref[i * 8 + u] + offset, 1), :] for u in range(8)], axis=0
            )
        return carry

    lax.fori_loop(0, count // 8, fetch, 0)

    def score(i, total):
        at = pl.multiple_of(i * 128, 128)
        anchor = a_ref[pl.ds(at, 128), :]
        positive = p_ref[pl.ds(at, 128), :]
        negative = n_ref[pl.ds(at, 128), :]
        gap = (
            jnp.sum(anchor * negative, axis=1, keepdims=True)
            - jnp.sum(anchor * positive, axis=1, keepdims=True)
        ) * inv_root
        soft = jnp.maximum(gap, 0.0) + jnp.log1p(jnp.exp(-jnp.abs(gap)))
        coef = jax.nn.sigmoid(gap) * (inv_root / loss_divisor)
        p_ref[pl.ds(at, 128), :] = coef * (negative - positive)
        a_ref[pl.ds(at, 128), :] = coef * anchor
        return total + jnp.sum(soft, axis=0, keepdims=True)

    total = lax.fori_loop(0, count // 128, score, jnp.zeros((1, 1), F32))
    loss_ref[...] = jnp.broadcast_to(total, loss_ref.shape)

    def spread(i, carry):
        for u in range(8):
            t = i * 8 + u
            moved = a_ref[pl.ds(t, 1), :]
            here = pl.ds(anchor_ref[t], 1)
            grad_anchor_ref[here, :] = grad_anchor_ref[here, :] + p_ref[pl.ds(t, 1), :]
            there = pl.ds(positive_ref[t], 1)
            grad_pos_ref[there, :] = grad_pos_ref[there, :] - moved
            away = pl.ds(negative_ref[t], 1)
            grad_neg_ref[away, :] = grad_neg_ref[away, :] + moved
        return carry

    lax.fori_loop(0, count // 8, spread, 0)

    for k, target in enumerate((gbelow_ref, gown_ref, gabove_ref, gsibling_ref, gcross_ref)):

        def merge(i, carry, k=k, target=target):
            at = pl.multiple_of(i * 256, 256)
            value = grad_pos_ref[pl.ds(k * hits + at, 256), :] + grad_neg_ref[
                pl.ds(k * hits + at, 256), :
            ]
            if k == 1:
                value = value + grad_anchor_ref[pl.ds(at, 256), :]
            target[pl.ds(at, 256), :] = value.astype(target.dtype)
            return carry

        lax.fori_loop(0, hits // 256, merge, 0)


def node_backward(
    gradient, hidden_ref, before_ref, agg_ref, w_out, gout_ref, gself_ref, gagg_ref, step
):
    upstream = gradient.astype(BF16)
    hidden = hidden_ref[...]
    hidden_grad = dot(upstream, w_out, 1, 1)
    act_grad = jnp.where(hidden.astype(F32) > 0, hidden_grad, 0.0).astype(BF16)

    @pl.when(step == 0)
    def _():
        gout_ref[...] = jnp.zeros(gout_ref.shape, F32)
        gself_ref[...] = jnp.zeros(gself_ref.shape, F32)
        gagg_ref[...] = jnp.zeros(gagg_ref.shape, F32)

    gout_ref[...] += dot(hidden, upstream, 0, 0)
    gself_ref[...] += dot(before_ref[...], act_grad, 0, 0)
    gagg_ref[...] += dot(agg_ref[...], act_grad, 0, 0)
    return act_grad


def spread_group(index_ref, tiles_ref, adj_ref, agg_grad_t, step, group, slots, rows):
    for g in range(group):
        tile = jnp.concatenate([tiles_ref[g, s] for s in range(slots)], axis=1)
        contrib = dot(agg_grad_t[:, g * rows : (g + 1) * rows], tile, 1, 0)
        for s in range(slots):
            at = index_ref[(step * group + g) * slots + s]
            adj_ref[at] = adj_ref[at] + contrib[:, s * rows : (s + 1) * rows]


def clear_blocks(adj_ref):
    def clear(i, carry):
        adj_ref[i] = jnp.zeros(adj_ref.shape[1:], F32)
        return carry

    lax.fori_loop(0, adj_ref.shape[0], clear, 0)


def last_backward(
    group,
    steps,
    index_ref,
    tiles_ref,
    own_ref,
    total_ref,
    sib_ref,
    hidden_ref,
    before_ref,
    agg_ref,
    w_self_ref,
    w_agg_ref,
    w_out_ref,
    gout_ref,
    gself_ref,
    gagg_ref,
    direct_ref,
    obelow_ref,
    oown_ref,
    oabove_ref,
    osibling_ref,
    ocross_ref,
    adj_ref,
):
    step = pl.program_id(0)
    slots, rows = tiles_ref.shape[1], tiles_ref.shape[2]

    @pl.when(step == 0)
    def _():
        clear_blocks(adj_ref)

    gradient = own_ref[...] + (
        total_ref[...].astype(F32) + sib_ref[...].astype(F32)
    )
    act_grad = node_backward(
        gradient, hidden_ref, before_ref, agg_ref, w_out_ref[...], gout_ref, gself_ref, gagg_ref, step
    )
    direct_ref[...] = gradient + dot(act_grad, w_self_ref[...], 1, 1)
    agg_grad_t = dot(w_agg_ref[...], act_grad, 1, 1).astype(BF16)
    spread_group(index_ref, tiles_ref, adj_ref, agg_grad_t, step, group, slots, rows)

    @pl.when(step == steps - 1)
    def _():
        blocks = oown_ref.shape[0]
        for k, target in enumerate((obelow_ref, oown_ref, oabove_ref, osibling_ref, ocross_ref)):

            def store(i, carry, k=k, target=target):
                target[i] = adj_ref[k * blocks + i].astype(target.dtype)
                return carry

            lax.fori_loop(0, blocks, store, 0)


def first_backward(
    group,
    steps,
    index_ref,
    tiles_ref,
    direct_ref,
    own_ref,
    total_ref,
    sib_ref,
    hidden_ref,
    before_ref,
    agg_ref,
    w_self_ref,
    w_agg_ref,
    w_out_ref,
    feats_ref,
    wcat_ref,
    wcat_t_ref,
    gout_ref,
    gself_ref,
    gagg_ref,
    genc_ref,
    adj_ref,
):
    step = pl.program_id(0)
    slots, rows = tiles_ref.shape[1], tiles_ref.shape[2]
    span = group * rows
    total = feats_ref.shape[1]

    @pl.when(step == 0)
    def _():
        clear_blocks(adj_ref)
        genc_ref[...] = jnp.zeros(genc_ref.shape, F32)

    pieces = []
    for g in range(group):
        returned = own_ref[g] + (
            total_ref[g].astype(F32) + sib_ref[g].astype(F32)
        )
        pieces.append(returned.T)
    gradient = direct_ref[...] + jnp.concatenate(pieces, axis=0)
    act_grad = node_backward(
        gradient, hidden_ref, before_ref, agg_ref, w_out_ref[...], gout_ref, gself_ref, gagg_ref, step
    )
    direct = gradient + dot(act_grad, w_self_ref[...], 1, 1)
    here = feats_ref[:, pl.ds(pl.multiple_of(total // 5 + step * span, span), span)]
    squashed = jnp.tanh(dot(here, wcat_ref[...], 0, 0))
    genc_ref[...] += dot(here, (direct * (1.0 - squashed * squashed)).astype(BF16), 1, 0)
    agg_grad_t = dot(w_agg_ref[...], act_grad, 1, 1).astype(BF16)
    spread_group(index_ref, tiles_ref, adj_ref, agg_grad_t, step, group, slots, rows)

    @pl.when(step == steps - 1)
    def _():
        per = 4

        def encode(i, carry):
            at = pl.multiple_of(i * (per * rows), per * rows)
            feats = feats_ref[:, pl.ds(at, per * rows)]
            squashed_t = jnp.tanh(dot(wcat_t_ref[...], feats, 1, 0))
            grad_t = jnp.concatenate([adj_ref[i * per + u] for u in range(per)], axis=1)
            grad_t = (grad_t * (1.0 - squashed_t * squashed_t)).astype(BF16)
            return carry + dot(feats, grad_t, 1, 1)

        genc_ref[...] += lax.fori_loop(
            0, total // (per * rows), encode, jnp.zeros(genc_ref.shape, F32)
        )


def body(
    hit_feats,
    layer_ids,
    edge_tiles,
    src_blocks,
    live_slots,
    anchor_hits,
    positive_hits,
    negative_hits,
    w_enc,
    layer_table,
    w_self,
    w_agg,
    w_out,
):
    blocks, slots, rows, _ = edge_tiles.shape
    width = w_enc.shape[1]
    features = hit_feats.shape[0]
    kinds = layer_table.shape[0]
    hits = blocks * rows
    layer_total = w_self.shape[0]
    triplets = anchor_hits.shape[0]
    group = 4
    steps = blocks // group
    span = group * rows
    me = lax.axis_index("phi")
    is_even = me % 2 == 0
    even_pair = (me // 2) % 2 == 0

    def place(part):
        spots = (
            jnp.where(even_pair, 2, 0),
            jnp.where(is_even, 4, 3),
            1,
            jnp.where(is_even, 3, 4),
            jnp.where(even_pair, 0, 2),
        )
        return sum(jnp.where(part == k, spot, 0) for k, spot in enumerate(spots))

    live = jnp.arange(slots, dtype=jnp.int32)[None, :] < live_slots[:, None]
    index = jnp.where(
        live, place(src_blocks // blocks) * blocks + src_blocks % blocks, 5 * blocks
    ).reshape(blocks * slots)
    positive = place(positive_hits // hits) * hits + positive_hits % hits
    negative = place(negative_hits // hits) * hits + negative_hits % hits

    pad = -(features + 1) % 16
    packed = jnp.concatenate(
        [hit_feats, layer_ids.astype(BF16)[None, :], jnp.zeros((pad, hits), BF16)], axis=0
    )
    packed = jnp.concatenate(
        [
            permute(packed, direct_target),
            packed,
            permute(packed, relayed_target),
            permute(packed, sibling_target),
            permute(packed, cross_target),
        ],
        axis=1,
    )
    feature_pad = -features % 16
    onehot = (
        jnp.arange(kinds, dtype=jnp.int32)[:, None].astype(BF16) == packed[features][None, :]
    ).astype(BF16)
    feats = jnp.concatenate(
        [packed[:features], jnp.zeros((feature_pad, 5 * hits), BF16), onehot], axis=0
    )
    wcat = jnp.concatenate([w_enc, jnp.zeros((feature_pad, width), BF16), layer_table], axis=0)
    depth = wcat.shape[0]

    tile_spec = pl.BlockSpec((group, slots, rows, rows), lambda i, *_: (i, 0, 0, 0))
    row_spec = pl.BlockSpec((span, width), lambda i, *_: (i, 0))
    block_spec = pl.BlockSpec((group, width, rows), lambda i, *_: (i, 0, 0))
    weight_spec = full((width, width))
    any_spec = pl.BlockSpec(memory_space=pl.ANY)
    row_shape = jax.ShapeDtypeStruct((hits, width), BF16)
    weight_shape = jax.ShapeDtypeStruct((width, width), F32)

    before0, agg0, hidden0, latents = pl.pallas_call(
        functools.partial(first_forward, group),
        grid_spec=pltpu.PrefetchScalarGridSpec(
            num_scalar_prefetch=1,
            grid=(steps,),
            in_specs=[tile_spec, full((depth, 5 * hits)), full((depth, width))] + [weight_spec] * 3,
            out_specs=[row_spec] * 4,
            scratch_shapes=[pltpu.VMEM((5 * hits + rows, width), BF16)],
        ),
        out_shape=[row_shape] * 4,
        compiler_params=params(),
        name="first_forward",
    )(index, edge_tiles, feats, wcat, w_self[0], w_agg[0], w_out[0])
    stored = [(before0, agg0, hidden0)]
    for layer in range(1, layer_total):
        pieces = window_pieces(latents)
        aggregated, hidden, updated = pl.pallas_call(
            functools.partial(later_forward, group),
            grid_spec=pltpu.PrefetchScalarGridSpec(
                num_scalar_prefetch=1,
                grid=(steps,),
                in_specs=[tile_spec] + [any_spec] * 5 + [weight_spec] * 3,
                out_specs=[row_spec] * 3,
                scratch_shapes=[
                    pltpu.VMEM((5 * hits + rows, width), BF16),
                    pltpu.SemaphoreType.DMA((5,)),
                ],
            ),
            out_shape=[row_shape] * 3,
            compiler_params=params(),
            name="later_forward",
        )(index, edge_tiles, *pieces, w_self[layer], w_agg[layer], w_out[layer])
        stored.append((latents, aggregated, hidden))
        latents = updated

    pieces = window_pieces(latents)
    wide_shape = jax.ShapeDtypeStruct((hits, width), F32)
    whole = full((hits, width))
    loss_part, gbelow, gown, gabove, gsibling, gcross = pl.pallas_call(
        functools.partial(contrast_kernel, 1.0 / math.sqrt(width)),
        grid_spec=pltpu.PrefetchScalarGridSpec(
            num_scalar_prefetch=3,
            grid=(1,),
            in_specs=[pl.BlockSpec((hits, width), lambda *_: (0, 0), pipeline_mode=pl.Buffered(1))] * 5,
            out_specs=[full((8, width))]
            + [pl.BlockSpec((hits, width), lambda *_: (0, 0), pipeline_mode=pl.Buffered(1))] * 5,
            scratch_shapes=[pltpu.VMEM((5 * hits, width), F32)] * 3
            + [pltpu.VMEM((hits, width), F32)]
            + [pltpu.VMEM((triplets, width), F32)] * 3,
        ),
        out_shape=[jax.ShapeDtypeStruct((8, width), F32)]
        + [wide_shape] * 3
        + [row_shape] * 2,
        compiler_params=params(),
        name="contrast",
    )(anchor_hits, positive, negative, *pieces)
    total, sib = return_pieces(gbelow, gabove, gsibling, gcross)

    t_shape = jax.ShapeDtypeStruct((blocks, width, rows), F32)
    t_half = jax.ShapeDtypeStruct((blocks, width, rows), BF16)
    t_full = pl.BlockSpec(
        (blocks, width, rows), lambda *_: (0, 0, 0), pipeline_mode=pl.Buffered(1)
    )
    adj_shape = pltpu.VMEM((5 * blocks + 1, width, rows), F32)
    own = gown
    before, aggregated, hidden = stored[1]
    gout1, gself1, gagg1, direct, obelow, own, oabove, osibling, ocross = pl.pallas_call(
        functools.partial(last_backward, group, steps),
        grid_spec=pltpu.PrefetchScalarGridSpec(
            num_scalar_prefetch=1,
            grid=(steps,),
            in_specs=[tile_spec] + [row_spec] * 6 + [weight_spec] * 3,
            out_specs=[weight_spec] * 3 + [row_spec] + [t_full] * 5,
            scratch_shapes=[adj_shape],
        ),
        out_shape=[weight_shape] * 3 + [wide_shape] + [t_shape] * 3 + [t_half] * 2,
        compiler_params=params(),
        name="last_backward",
    )(
        index, edge_tiles, own, total, sib, hidden, before, aggregated,
        w_self[1], w_agg[1], w_out[1],
    )
    total, sib = return_pieces(obelow, oabove, osibling, ocross)
    before, aggregated, hidden = stored[0]
    gout0, gself0, gagg0, genc = pl.pallas_call(
        functools.partial(first_backward, group, steps),
        grid_spec=pltpu.PrefetchScalarGridSpec(
            num_scalar_prefetch=1,
            grid=(steps,),
            in_specs=[tile_spec, row_spec]
            + [block_spec] * 3
            + [row_spec] * 3
            + [weight_spec] * 3
            + [full((depth, 5 * hits)), full((depth, width)), full((width, depth))],
            out_specs=[weight_spec] * 3 + [full((depth, width))],
            scratch_shapes=[adj_shape],
        ),
        out_shape=[weight_shape] * 3 + [jax.ShapeDtypeStruct((depth, width), F32)],
        compiler_params=params(),
        name="first_backward",
    )(
        index, edge_tiles, direct, own, total, sib, hidden, before, aggregated,
        w_self[0], w_agg[0], w_out[0], feats, wcat, wcat.T,
    )
    late = sum_all(
        jnp.concatenate([gout0, gout1, gself0, gself1, gagg0, gagg1, genc, loss_part], axis=0)
    )

    triplet_total = triplets * lax.axis_size("phi")
    base = 6 * width
    loss = (late[base + depth, 0] / triplet_total).reshape(1)
    grad_enc = late[base : base + features]
    grad_table = late[base + depth - kinds : base + depth]

    def pair(k):
        return late[2 * k * width : 2 * (k + 1) * width].reshape(layer_total, width, width)

    return (loss, grad_enc, grad_table, pair(1), pair(2), pair(0))


def solution(mesh):
    both = ("event", "phi")
    in_specs = (
        P(None, both),
        P(both),
        P(both, None, None, None),
        P(both, None),
        P(both),
        P(both),
        P(both),
        P(both),
        P(),
        P(),
        P(),
        P(),
        P(),
    )
    out_specs = (
        P("event"),
        P("event", None),
        P("event", None),
        P("event", None, None),
        P("event", None, None),
        P("event", None, None),
    )
    return jax.shard_map(body, mesh=mesh, in_specs=in_specs, out_specs=out_specs, check_vma=False)
```

```python
import functools
import math

import jax
import jax.numpy as jnp
from jax import lax
from jax.experimental import pallas as pl
from jax.experimental.pallas import tpu as pltpu
from jax.sharding import PartitionSpec as P

loss_divisor = 64.0
F32 = jnp.float32
BF16 = jnp.bfloat16
VMEM_BYTES = 60 * 1024 * 1024


def dot(left, right, left_dim, right_dim):
    return lax.dot_general(
        left, right, (((left_dim,), (right_dim,)), ((), ())), preferred_element_type=F32
    )


def full(shape):
    return pl.BlockSpec(shape, lambda *_: (0,) * len(shape))


def params():
    return pltpu.CompilerParams(
        dimension_semantics=("arbitrary",), vmem_limit_bytes=VMEM_BYTES
    )


CHUNKS = 16


def peers():
    count = lax.axis_size("phi")
    me = lax.axis_index("phi")
    odd_pair = (me // 2) % 2
    odd_core = me % 2
    direct = me + 2 - 4 * odd_pair
    sibling = me + 1 - 2 * odd_core
    stride = 4 - 8 * odd_pair
    onward = (me + stride + count) % count
    source = (me - stride + count) % count
    return direct, sibling, onward, source, odd_pair == odd_core


def remote(src, dst, send, recv, target):
    return pltpu.make_async_remote_copy(
        src_ref=src,
        dst_ref=dst,
        send_sem=send,
        recv_sem=recv,
        device_id={"phi": target},
        device_id_type=pl.DeviceIdType.MESH,
    )


def greet(targets):
    barrier = pltpu.get_barrier_semaphore()
    for target in targets:
        pl.semaphore_signal(
            barrier, inc=1, device_id={"phi": target}, device_id_type=pl.DeviceIdType.MESH
        )
    pl.semaphore_wait(barrier, len(targets))


def exchange_kernel(own, direct_out, relay_out, sib_out, cross_out, *sems):
    ys, yr, zs, zr, cs, cr, ss, sr = sems
    direct, sibling, onward, source, direct_crosses = peers()
    size = own.shape[0] // CHUNKS
    greet((direct, sibling, source))

    def part(ref, i):
        return ref.at[pl.ds(i * size, size)]

    first = [
        remote(part(own, i), part(direct_out, i), ys.at[i], yr.at[i], direct) for i in range(CHUNKS)
    ]
    second = [
        remote(part(direct_out, i), part(relay_out, i), zs.at[i], zr.at[i], onward)
        for i in range(CHUNKS)
    ]
    cross_a = [
        remote(part(direct_out, i), part(cross_out, i), cs.at[i], cr.at[i], sibling)
        for i in range(CHUNKS)
    ]
    cross_b = [
        remote(part(relay_out, i), part(cross_out, i), cs.at[i], cr.at[i], sibling)
        for i in range(CHUNKS)
    ]
    near = remote(own, sib_out, ss.at[0], sr.at[0], sibling)
    for copy in first:
        copy.start()
    near.start()
    for i in range(CHUNKS):
        first[i].wait_recv()
        second[i].start()

        @pl.when(direct_crosses)
        def _():
            cross_a[i].start()

    for i in range(CHUNKS):
        second[i].wait_recv()

        @pl.when(jnp.logical_not(direct_crosses))
        def _():
            cross_b[i].start()

    near.wait()
    for i in range(CHUNKS):
        first[i].wait_send()
        second[i].wait_send()
        cross_a[i].wait()


def feature_kernel(own_ref, out_ref, sends, recvs):
    count = lax.axis_size("phi")
    me = lax.axis_index("phi")
    odd_pair = (me // 2) % 2
    odd_core = me % 2
    far = (me - 2 + 4 * odd_pair + count) % count
    cross = (me - 1 + 2 * odd_core + count) % count
    direct = me + 2 - 4 * odd_pair
    sibling = me + 1 - 2 * odd_core
    hits = own_ref.shape[1]
    targets = (direct, far, sibling, cross)
    greet(targets)
    copies = [
        remote(
            own_ref,
            out_ref.at[:, pl.ds(place * hits, hits)],
            sends.at[k],
            recvs.at[k],
            targets[k],
        )
        for k, place in enumerate((0, 2, 3, 4))
    ]
    for copy in copies:
        copy.start()
    out_ref[:, pl.ds(hits, hits)] = own_ref[...]
    for copy in copies:
        copy.wait()


def feature_window(packed):
    depth, hits = packed.shape
    vmem = pl.BlockSpec(memory_space=pltpu.VMEM)
    return pl.pallas_call(
        feature_kernel,
        in_specs=[vmem],
        out_specs=vmem,
        out_shape=jax.ShapeDtypeStruct((depth, 5 * hits), BF16),
        scratch_shapes=[pltpu.SemaphoreType.DMA((4,))] * 2,
        compiler_params=pltpu.CompilerParams(collective_id=4, has_side_effects=True),
        name="features",
    )(packed)


def window_pieces(latents):
    hits, width = latents.shape
    any_spec = pl.BlockSpec(memory_space=pl.ANY)
    direct, relayed, sibling, cross = pl.pallas_call(
        exchange_kernel,
        in_specs=[any_spec],
        out_specs=[any_spec] * 4,
        out_shape=[jax.ShapeDtypeStruct((hits, width), BF16)] * 4,
        scratch_shapes=[pltpu.SemaphoreType.DMA((CHUNKS,))] * 6 + [pltpu.SemaphoreType.DMA((1,))] * 2,
        compiler_params=pltpu.CompilerParams(collective_id=1, has_side_effects=True),
        name="exchange",
    )(latents)
    return direct, latents, relayed, sibling, cross


def return_kernel(
    direct_ref,
    relay_ref,
    sib_ref,
    cross_ref,
    total_out,
    sib_out,
    cross_in,
    relay_send,
    relay_in,
    direct_send,
    *sems,
):
    ys, yr, zs, zr, cs, cr, ss, sr = sems
    direct, sibling, onward, source, to_direct = peers()
    size = direct_ref.shape[0] // CHUNKS
    greet((direct, sibling, onward))

    def rows(i):
        return pl.ds(i * size, size)

    crosses = [
        remote(cross_ref.at[rows(i)], cross_in.at[rows(i)], cs.at[i], cr.at[i], sibling)
        for i in range(CHUNKS)
    ]
    first = [
        remote(relay_send.at[rows(i)], relay_in.at[rows(i)], zs.at[i], zr.at[i], source)
        for i in range(CHUNKS)
    ]
    second = [
        remote(direct_send.at[rows(i)], total_out.at[rows(i)], ys.at[i], yr.at[i], direct)
        for i in range(CHUNKS)
    ]
    near = remote(sib_ref, sib_out, ss.at[0], sr.at[0], sibling)
    for copy in crosses:
        copy.start()
    near.start()
    for i in range(CHUNKS):
        crosses[i].wait_recv()
        extra = jnp.where(to_direct, 0.0, cross_in[rows(i), :].astype(F32))
        relay_send[rows(i), :] = (relay_ref[rows(i), :] + extra).astype(BF16)
        first[i].start()
    for i in range(CHUNKS):
        first[i].wait_recv()
        extra = jnp.where(to_direct, cross_in[rows(i), :].astype(F32), 0.0)
        direct_send[rows(i), :] = (
            direct_ref[rows(i), :] + extra + relay_in[rows(i), :].astype(F32)
        ).astype(BF16)
        second[i].start()
    near.wait()
    for i in range(CHUNKS):
        crosses[i].wait_send()
        first[i].wait_send()
        second[i].wait()


def return_pieces(direct, relayed, sibling, cross):
    shape = sibling.shape
    hits, width = math.prod(shape[:-1]), shape[-1]
    vmem = pl.BlockSpec(memory_space=pltpu.VMEM)
    half = jax.ShapeDtypeStruct((hits, width), BF16)
    total, sib = pl.pallas_call(
        return_kernel,
        in_specs=[vmem] * 4,
        out_specs=[vmem] * 2,
        out_shape=[half] * 2,
        scratch_shapes=[pltpu.VMEM((hits, width), BF16)] * 4
        + [pltpu.SemaphoreType.DMA((CHUNKS,))] * 6
        + [pltpu.SemaphoreType.DMA((1,))] * 2,
        compiler_params=pltpu.CompilerParams(
            collective_id=2, has_side_effects=True, vmem_limit_bytes=VMEM_BYTES
        ),
        name="give_back",
    )(*[piece.reshape(hits, width) for piece in (direct, relayed, sibling, cross)])
    return total.reshape(shape), sib.reshape(shape)


def sum_kernel(
    pairs, parts, *refs
):
    part_refs = refs[:parts]
    out_ref, x_ref, half_in, acc_ref, slots_in, all_ref, s0, r0, s1, r1, s2, r2, s3, r3 = refs[parts:]
    at = 0
    for part_ref in part_refs:
        x_ref[pl.ds(at, part_ref.shape[0]), :] = part_ref[...]
        at += part_ref.shape[0]
    if at < x_ref.shape[0]:
        x_ref[pl.ds(at, x_ref.shape[0] - at), :] = jnp.zeros((x_ref.shape[0] - at, x_ref.shape[1]), F32)
    me = lax.axis_index("phi")
    pair, core = me // 2, me % 2
    sibling = me + 1 - 2 * core
    half = x_ref.shape[0] // 2
    chunk = half // pairs
    others = [((pair + d) % pairs) * 2 + core for d in range(1, pairs)]
    greet([sibling] + others)

    def span(start, size):
        return pl.ds(pl.multiple_of(start, 8), size)

    swap = remote(x_ref.at[span((1 - core) * half, half)], half_in, s0.at[0], r0.at[0], sibling)
    swap.start()
    swap.wait()
    acc_ref[...] = x_ref[span(core * half, half), :] + half_in[...]
    scatter = [
        remote(
            acc_ref.at[span(((pair + d) % pairs) * chunk, chunk)],
            slots_in.at[d - 1],
            s1.at[d - 1],
            r1.at[d - 1],
            others[d - 1],
        )
        for d in range(1, pairs)
    ]
    for copy in scatter:
        copy.start()
    total = acc_ref[span(pair * chunk, chunk), :]
    for d in range(1, pairs):
        scatter[d - 1].wait_recv()
        total = total + slots_in[d - 1]
    mine = span(core * half + pair * chunk, chunk)
    all_ref[mine, :] = total
    gather = [
        remote(all_ref.at[mine], all_ref.at[mine], s2.at[d - 1], r2.at[d - 1], others[d - 1])
        for d in range(1, pairs)
    ]
    for copy in gather:
        copy.start()
    for copy in gather:
        copy.wait()
    for copy in scatter:
        copy.wait_send()
    whole = span(core * half, half)
    last = remote(all_ref.at[whole], all_ref.at[whole], s3.at[0], r3.at[0], sibling)
    last.start()
    last.wait()
    out_ref[...] = all_ref[...]


def sum_all(values):
    pairs = lax.axis_size("phi") // 2
    rows, width = sum(value.shape[0] for value in values), values[0].shape[1]
    chunk = -(-rows // (16 * pairs)) * 8
    total = 2 * pairs * chunk
    vmem = pl.BlockSpec(memory_space=pltpu.VMEM)
    one = pltpu.SemaphoreType.DMA((1,))
    many = pltpu.SemaphoreType.DMA((pairs - 1,))
    return pl.pallas_call(
        functools.partial(sum_kernel, pairs, len(values)),
        in_specs=[vmem] * len(values),
        out_specs=vmem,
        out_shape=jax.ShapeDtypeStruct((total, width), F32),
        scratch_shapes=[
            pltpu.VMEM((total, width), F32),
            pltpu.VMEM((total // 2, width), F32),
            pltpu.VMEM((total // 2, width), F32),
            pltpu.VMEM((pairs - 1, chunk, width), F32),
            pltpu.VMEM((total, width), F32),
            one, one, many, many, many, many, one, one,
        ],
        compiler_params=pltpu.CompilerParams(
            collective_id=3, has_side_effects=True, vmem_limit_bytes=VMEM_BYTES
        ),
        name="sum_all",
    )(*values)


def aggregate_group(index_ref, tiles_ref, window_ref, step, group, slots, rows):
    results = []
    for g in range(group):
        tile = jnp.concatenate([tiles_ref[g, s] for s in range(slots)], axis=1)
        source = jnp.concatenate(
            [
                window_ref[
                    pl.ds(
                        pl.multiple_of(index_ref[(step * group + g) * slots + s] * rows, rows),
                        rows,
                    ),
                    :,
                ]
                for s in range(slots)
            ],
            axis=0,
        )
        results.append(dot(tile, source, 1, 0).astype(BF16))
    return jnp.concatenate(results, axis=0)


def node_update(own, aggregated, w_self, w_agg, w_out):
    activation = dot(own, w_self, 1, 0) + dot(aggregated, w_agg, 1, 0)
    hidden = jnp.maximum(activation, 0.0).astype(BF16)
    updated = (own.astype(F32) + dot(hidden, w_out, 1, 0)).astype(BF16)
    return hidden, updated


def first_forward(
    group,
    index_ref,
    tiles_ref,
    feats_ref,
    wcat_ref,
    w_self_ref,
    w_agg_ref,
    w_out_ref,
    before_ref,
    agg_ref,
    hidden_ref,
    updated_ref,
    window_ref,
):
    step = pl.program_id(0)
    slots, rows = tiles_ref.shape[1], tiles_ref.shape[2]
    span = group * rows
    total = feats_ref.shape[1]

    @pl.when(step == 0)
    def _():
        def encode(i, carry):
            at = pl.multiple_of(i * 512, 512)
            encoded = dot(feats_ref[:, pl.ds(at, 512)], wcat_ref[...], 0, 0)
            window_ref[pl.ds(at, 512), :] = jnp.tanh(encoded).astype(BF16)
            return carry

        lax.fori_loop(0, total // 512, encode, 0)
        window_ref[pl.ds(total, rows), :] = jnp.zeros((rows, window_ref.shape[1]), BF16)

    aggregated = aggregate_group(index_ref, tiles_ref, window_ref, step, group, slots, rows)
    own = window_ref[pl.ds(pl.multiple_of(total // 5 + step * span, span), span), :]
    hidden, updated = node_update(own, aggregated, w_self_ref[...], w_agg_ref[...], w_out_ref[...])
    before_ref[...] = own
    agg_ref[...] = aggregated
    hidden_ref[...] = hidden
    updated_ref[...] = updated


def later_forward(
    group,
    index_ref,
    tiles_ref,
    below_ref,
    own_ref,
    above_ref,
    sibling_ref,
    cross_ref,
    w_self_ref,
    w_agg_ref,
    w_out_ref,
    agg_ref,
    hidden_ref,
    updated_ref,
    window_ref,
    sems,
):
    step = pl.program_id(0)
    slots, rows = tiles_ref.shape[1], tiles_ref.shape[2]
    span = group * rows
    hits = own_ref.shape[0]

    @pl.when(step == 0)
    def _():
        copies = [
            pltpu.make_async_copy(piece, window_ref.at[pl.ds(k * hits, hits)], sems.at[k])
            for k, piece in enumerate((below_ref, own_ref, above_ref, sibling_ref, cross_ref))
        ]
        for copy in copies:
            copy.start()
        window_ref[pl.ds(5 * hits, rows), :] = jnp.zeros((rows, window_ref.shape[1]), BF16)
        for copy in copies:
            copy.wait()

    aggregated = aggregate_group(index_ref, tiles_ref, window_ref, step, group, slots, rows)
    own = window_ref[pl.ds(pl.multiple_of(hits + step * span, span), span), :]
    hidden, updated = node_update(own, aggregated, w_self_ref[...], w_agg_ref[...], w_out_ref[...])
    agg_ref[...] = aggregated
    hidden_ref[...] = hidden
    updated_ref[...] = updated


def contrast_kernel(
    inv_root,
    anchor_ref,
    positive_ref,
    negative_ref,
    below_ref,
    own_ref,
    above_ref,
    sibling_ref,
    cross_ref,
    loss_ref,
    gbelow_ref,
    gown_ref,
    gabove_ref,
    gsibling_ref,
    gcross_ref,
    window_ref,
    grad_pos_ref,
    grad_neg_ref,
    grad_anchor_ref,
    a_ref,
    p_ref,
    n_ref,
):
    hits = own_ref.shape[0]
    count = a_ref.shape[0]
    width = own_ref.shape[1]
    for k, piece in enumerate((below_ref, own_ref, above_ref, sibling_ref, cross_ref)):

        def widen(i, carry, k=k, piece=piece):
            at = pl.multiple_of(i * 256, 256)
            window_ref[pl.ds(k * hits + at, 256), :] = piece[pl.ds(at, 256), :].astype(F32)
            zeros = jnp.zeros((256, width), F32)
            grad_pos_ref[pl.ds(k * hits + at, 256), :] = zeros
            grad_neg_ref[pl.ds(k * hits + at, 256), :] = zeros
            if k == 0:
                grad_anchor_ref[pl.ds(at, 256), :] = zeros
            return carry

        lax.fori_loop(0, hits // 256, widen, 0)

    def fetch(i, carry):
        at = pl.multiple_of(i * 8, 8)
        for index_ref, offset, target in (
            (anchor_ref, hits, a_ref),
            (positive_ref, 0, p_ref),
            (negative_ref, 0, n_ref),
        ):
            target[pl.ds(at, 8), :] = jnp.concatenate(
                [window_ref[pl.ds(index_ref[i * 8 + u] + offset, 1), :] for u in range(8)], axis=0
            )
        return carry

    lax.fori_loop(0, count // 8, fetch, 0)

    def score(i, total):
        at = pl.multiple_of(i * 128, 128)
        anchor = a_ref[pl.ds(at, 128), :]
        positive = p_ref[pl.ds(at, 128), :]
        negative = n_ref[pl.ds(at, 128), :]
        gap = (
            jnp.sum(anchor * negative, axis=1, keepdims=True)
            - jnp.sum(anchor * positive, axis=1, keepdims=True)
        ) * inv_root
        soft = jnp.maximum(gap, 0.0) + jnp.log1p(jnp.exp(-jnp.abs(gap)))
        coef = jax.nn.sigmoid(gap) * (inv_root / loss_divisor)
        p_ref[pl.ds(at, 128), :] = coef * (negative - positive)
        a_ref[pl.ds(at, 128), :] = coef * anchor
        return total + jnp.sum(soft, axis=0, keepdims=True)

    total = lax.fori_loop(0, count // 128, score, jnp.zeros((1, 1), F32))
    loss_ref[...] = jnp.broadcast_to(total, loss_ref.shape)

    def spread(i, carry):
        for u in range(8):
            t = i * 8 + u
            moved = a_ref[pl.ds(t, 1), :]
            here = pl.ds(anchor_ref[t], 1)
            grad_anchor_ref[here, :] = grad_anchor_ref[here, :] + p_ref[pl.ds(t, 1), :]
            there = pl.ds(positive_ref[t], 1)
            grad_pos_ref[there, :] = grad_pos_ref[there, :] - moved
            away = pl.ds(negative_ref[t], 1)
            grad_neg_ref[away, :] = grad_neg_ref[away, :] + moved
        return carry

    lax.fori_loop(0, count // 8, spread, 0)

    for k, target in enumerate((gbelow_ref, gown_ref, gabove_ref, gsibling_ref, gcross_ref)):

        def merge(i, carry, k=k, target=target):
            at = pl.multiple_of(i * 256, 256)
            value = grad_pos_ref[pl.ds(k * hits + at, 256), :] + grad_neg_ref[
                pl.ds(k * hits + at, 256), :
            ]
            if k == 1:
                value = value + grad_anchor_ref[pl.ds(at, 256), :]
            target[pl.ds(at, 256), :] = value.astype(target.dtype)
            return carry

        lax.fori_loop(0, hits // 256, merge, 0)


def node_backward(
    gradient, hidden_ref, before_ref, agg_ref, w_out, gout_ref, gself_ref, gagg_ref, step
):
    upstream = gradient.astype(BF16)
    hidden = hidden_ref[...]
    hidden_grad = dot(upstream, w_out, 1, 1)
    act_grad = jnp.where(hidden.astype(F32) > 0, hidden_grad, 0.0).astype(BF16)

    @pl.when(step == 0)
    def _():
        gout_ref[...] = jnp.zeros(gout_ref.shape, F32)
        gself_ref[...] = jnp.zeros(gself_ref.shape, F32)
        gagg_ref[...] = jnp.zeros(gagg_ref.shape, F32)

    gout_ref[...] += dot(hidden, upstream, 0, 0)
    gself_ref[...] += dot(before_ref[...], act_grad, 0, 0)
    gagg_ref[...] += dot(agg_ref[...], act_grad, 0, 0)
    return act_grad


def spread_group(index_ref, tiles_ref, adj_ref, agg_grad_t, step, group, slots, rows):
    for g in range(group):
        tile = jnp.concatenate([tiles_ref[g, s] for s in range(slots)], axis=1)
        contrib = dot(agg_grad_t[:, g * rows : (g + 1) * rows], tile, 1, 0)
        for s in range(slots):
            at = index_ref[(step * group + g) * slots + s]
            adj_ref[at] = adj_ref[at] + contrib[:, s * rows : (s + 1) * rows]


def clear_blocks(adj_ref):
    def clear(i, carry):
        adj_ref[i] = jnp.zeros(adj_ref.shape[1:], F32)
        return carry

    lax.fori_loop(0, adj_ref.shape[0], clear, 0)


def last_backward(
    group,
    steps,
    index_ref,
    tiles_ref,
    own_ref,
    total_ref,
    sib_ref,
    hidden_ref,
    before_ref,
    agg_ref,
    w_self_ref,
    w_agg_ref,
    w_out_ref,
    gout_ref,
    gself_ref,
    gagg_ref,
    direct_ref,
    obelow_ref,
    oown_ref,
    oabove_ref,
    osibling_ref,
    ocross_ref,
    adj_ref,
):
    step = pl.program_id(0)
    slots, rows = tiles_ref.shape[1], tiles_ref.shape[2]

    @pl.when(step == 0)
    def _():
        clear_blocks(adj_ref)

    gradient = own_ref[...] + (
        total_ref[...].astype(F32) + sib_ref[...].astype(F32)
    )
    act_grad = node_backward(
        gradient, hidden_ref, before_ref, agg_ref, w_out_ref[...], gout_ref, gself_ref, gagg_ref, step
    )
    direct_ref[...] = gradient + dot(act_grad, w_self_ref[...], 1, 1)
    agg_grad_t = dot(w_agg_ref[...], act_grad, 1, 1).astype(BF16)
    spread_group(index_ref, tiles_ref, adj_ref, agg_grad_t, step, group, slots, rows)

    @pl.when(step == steps - 1)
    def _():
        blocks = oown_ref.shape[0]
        for k, target in enumerate((obelow_ref, oown_ref, oabove_ref, osibling_ref, ocross_ref)):

            def store(i, carry, k=k, target=target):
                target[i] = adj_ref[k * blocks + i].astype(target.dtype)
                return carry

            lax.fori_loop(0, blocks, store, 0)


def first_backward(
    group,
    steps,
    index_ref,
    tiles_ref,
    direct_ref,
    own_ref,
    total_ref,
    sib_ref,
    hidden_ref,
    before_ref,
    agg_ref,
    w_self_ref,
    w_agg_ref,
    w_out_ref,
    feats_ref,
    wcat_ref,
    wcat_t_ref,
    gout_ref,
    gself_ref,
    gagg_ref,
    genc_ref,
    adj_ref,
):
    step = pl.program_id(0)
    slots, rows = tiles_ref.shape[1], tiles_ref.shape[2]
    span = group * rows
    total = feats_ref.shape[1]

    @pl.when(step == 0)
    def _():
        clear_blocks(adj_ref)
        genc_ref[...] = jnp.zeros(genc_ref.shape, F32)

    pieces = []
    for g in range(group):
        returned = own_ref[g] + (
            total_ref[g].astype(F32) + sib_ref[g].astype(F32)
        )
        pieces.append(returned.T)
    gradient = direct_ref[...] + jnp.concatenate(pieces, axis=0)
    act_grad = node_backward(
        gradient, hidden_ref, before_ref, agg_ref, w_out_ref[...], gout_ref, gself_ref, gagg_ref, step
    )
    direct = gradient + dot(act_grad, w_self_ref[...], 1, 1)
    here = feats_ref[:, pl.ds(pl.multiple_of(total // 5 + step * span, span), span)]
    squashed = jnp.tanh(dot(here, wcat_ref[...], 0, 0))
    genc_ref[...] += dot(here, (direct * (1.0 - squashed * squashed)).astype(BF16), 1, 0)
    agg_grad_t = dot(w_agg_ref[...], act_grad, 1, 1).astype(BF16)
    spread_group(index_ref, tiles_ref, adj_ref, agg_grad_t, step, group, slots, rows)

    @pl.when(step == steps - 1)
    def _():
        per = 4

        def encode(i, carry):
            at = pl.multiple_of(i * (per * rows), per * rows)
            feats = feats_ref[:, pl.ds(at, per * rows)]
            squashed_t = jnp.tanh(dot(wcat_t_ref[...], feats, 1, 0))
            grad_t = jnp.concatenate([adj_ref[i * per + u] for u in range(per)], axis=1)
            grad_t = (grad_t * (1.0 - squashed_t * squashed_t)).astype(BF16)
            return carry + dot(feats, grad_t, 1, 1)

        genc_ref[...] += lax.fori_loop(
            0, total // (per * rows), encode, jnp.zeros(genc_ref.shape, F32)
        )


def body(
    hit_feats,
    layer_ids,
    edge_tiles,
    src_blocks,
    live_slots,
    anchor_hits,
    positive_hits,
    negative_hits,
    w_enc,
    layer_table,
    w_self,
    w_agg,
    w_out,
):
    blocks, slots, rows, _ = edge_tiles.shape
    width = w_enc.shape[1]
    features = hit_feats.shape[0]
    kinds = layer_table.shape[0]
    hits = blocks * rows
    layer_total = w_self.shape[0]
    triplets = anchor_hits.shape[0]
    group = 4
    steps = blocks // group
    span = group * rows
    me = lax.axis_index("phi")
    is_even = me % 2 == 0
    even_pair = (me // 2) % 2 == 0

    def place(part):
        spots = (
            jnp.where(even_pair, 2, 0),
            jnp.where(is_even, 4, 3),
            1,
            jnp.where(is_even, 3, 4),
            jnp.where(even_pair, 0, 2),
        )
        return sum(jnp.where(part == k, spot, 0) for k, spot in enumerate(spots))

    live = jnp.arange(slots, dtype=jnp.int32)[None, :] < live_slots[:, None]
    index = jnp.where(
        live, place(src_blocks // blocks) * blocks + src_blocks % blocks, 5 * blocks
    ).reshape(blocks * slots)
    positive = place(positive_hits // hits) * hits + positive_hits % hits
    negative = place(negative_hits // hits) * hits + negative_hits % hits

    pad = -(features + 1) % 16
    packed = jnp.concatenate(
        [hit_feats, layer_ids.astype(BF16)[None, :], jnp.zeros((pad, hits), BF16)], axis=0
    )
    packed = feature_window(packed)
    feature_pad = -features % 16
    onehot = (
        jnp.arange(kinds, dtype=jnp.int32)[:, None].astype(BF16) == packed[features][None, :]
    ).astype(BF16)
    feats = jnp.concatenate(
        [packed[:features], jnp.zeros((feature_pad, 5 * hits), BF16), onehot], axis=0
    )
    wcat = jnp.concatenate([w_enc, jnp.zeros((feature_pad, width), BF16), layer_table], axis=0)
    depth = wcat.shape[0]

    tile_spec = pl.BlockSpec((group, slots, rows, rows), lambda i, *_: (i, 0, 0, 0))
    row_spec = pl.BlockSpec((span, width), lambda i, *_: (i, 0))
    block_spec = pl.BlockSpec((group, width, rows), lambda i, *_: (i, 0, 0))
    weight_spec = full((width, width))
    any_spec = pl.BlockSpec(memory_space=pl.ANY)
    row_shape = jax.ShapeDtypeStruct((hits, width), BF16)
    weight_shape = jax.ShapeDtypeStruct((width, width), F32)

    before0, agg0, hidden0, latents = pl.pallas_call(
        functools.partial(first_forward, group),
        grid_spec=pltpu.PrefetchScalarGridSpec(
            num_scalar_prefetch=1,
            grid=(steps,),
            in_specs=[tile_spec, full((depth, 5 * hits)), full((depth, width))] + [weight_spec] * 3,
            out_specs=[row_spec] * 4,
            scratch_shapes=[pltpu.VMEM((5 * hits + rows, width), BF16)],
        ),
        out_shape=[row_shape] * 4,
        compiler_params=params(),
        name="first_forward",
    )(index, edge_tiles, feats, wcat, w_self[0], w_agg[0], w_out[0])
    stored = [(before0, agg0, hidden0)]
    for layer in range(1, layer_total):
        pieces = window_pieces(latents)
        aggregated, hidden, updated = pl.pallas_call(
            functools.partial(later_forward, group),
            grid_spec=pltpu.PrefetchScalarGridSpec(
                num_scalar_prefetch=1,
                grid=(steps,),
                in_specs=[tile_spec] + [any_spec] * 5 + [weight_spec] * 3,
                out_specs=[row_spec] * 3,
                scratch_shapes=[
                    pltpu.VMEM((5 * hits + rows, width), BF16),
                    pltpu.SemaphoreType.DMA((5,)),
                ],
            ),
            out_shape=[row_shape] * 3,
            compiler_params=params(),
            name="later_forward",
        )(index, edge_tiles, *pieces, w_self[layer], w_agg[layer], w_out[layer])
        stored.append((latents, aggregated, hidden))
        latents = updated

    pieces = window_pieces(latents)
    wide_shape = jax.ShapeDtypeStruct((hits, width), F32)
    whole = full((hits, width))
    loss_part, gbelow, gown, gabove, gsibling, gcross = pl.pallas_call(
        functools.partial(contrast_kernel, 1.0 / math.sqrt(width)),
        grid_spec=pltpu.PrefetchScalarGridSpec(
            num_scalar_prefetch=3,
            grid=(1,),
            in_specs=[pl.BlockSpec((hits, width), lambda *_: (0, 0), pipeline_mode=pl.Buffered(1))] * 5,
            out_specs=[full((8, width))]
            + [pl.BlockSpec((hits, width), lambda *_: (0, 0), pipeline_mode=pl.Buffered(1))] * 5,
            scratch_shapes=[pltpu.VMEM((5 * hits, width), F32)] * 3
            + [pltpu.VMEM((hits, width), F32)]
            + [pltpu.VMEM((triplets, width), F32)] * 3,
        ),
        out_shape=[jax.ShapeDtypeStruct((8, width), F32)]
        + [wide_shape] * 3
        + [row_shape] * 2,
        compiler_params=params(),
        name="contrast",
    )(anchor_hits, positive, negative, *pieces)
    total, sib = return_pieces(gbelow, gabove, gsibling, gcross)

    t_shape = jax.ShapeDtypeStruct((blocks, width, rows), F32)
    t_half = jax.ShapeDtypeStruct((blocks, width, rows), BF16)
    t_full = pl.BlockSpec(
        (blocks, width, rows), lambda *_: (0, 0, 0), pipeline_mode=pl.Buffered(1)
    )
    adj_shape = pltpu.VMEM((5 * blocks + 1, width, rows), F32)
    own = gown
    before, aggregated, hidden = stored[1]
    gout1, gself1, gagg1, direct, obelow, own, oabove, osibling, ocross = pl.pallas_call(
        functools.partial(last_backward, group, steps),
        grid_spec=pltpu.PrefetchScalarGridSpec(
            num_scalar_prefetch=1,
            grid=(steps,),
            in_specs=[tile_spec] + [row_spec] * 6 + [weight_spec] * 3,
            out_specs=[weight_spec] * 3 + [row_spec] + [t_full] * 5,
            scratch_shapes=[adj_shape],
        ),
        out_shape=[weight_shape] * 3 + [wide_shape] + [t_shape] * 3 + [t_half] * 2,
        compiler_params=params(),
        name="last_backward",
    )(
        index, edge_tiles, own, total, sib, hidden, before, aggregated,
        w_self[1], w_agg[1], w_out[1],
    )
    total, sib = return_pieces(obelow, oabove, osibling, ocross)
    before, aggregated, hidden = stored[0]
    gout0, gself0, gagg0, genc = pl.pallas_call(
        functools.partial(first_backward, group, steps),
        grid_spec=pltpu.PrefetchScalarGridSpec(
            num_scalar_prefetch=1,
            grid=(steps,),
            in_specs=[tile_spec, row_spec]
            + [block_spec] * 3
            + [row_spec] * 3
            + [weight_spec] * 3
            + [full((depth, 5 * hits)), full((depth, width)), full((width, depth))],
            out_specs=[weight_spec] * 3 + [full((depth, width))],
            scratch_shapes=[adj_shape],
        ),
        out_shape=[weight_shape] * 3 + [jax.ShapeDtypeStruct((depth, width), F32)],
        compiler_params=params(),
        name="first_backward",
    )(
        index, edge_tiles, direct, own, total, sib, hidden, before, aggregated,
        w_self[0], w_agg[0], w_out[0], feats, wcat, wcat.T,
    )
    late = sum_all([gout0, gout1, gself0, gself1, gagg0, gagg1, genc, loss_part])

    triplet_total = triplets * lax.axis_size("phi")
    base = 6 * width
    loss = (late[base + depth, 0] / triplet_total).reshape(1)
    grad_enc = late[base : base + features]
    grad_table = late[base + depth - kinds : base + depth]

    def pair(k):
        return late[2 * k * width : 2 * (k + 1) * width].reshape(layer_total, width, width)

    return (loss, grad_enc, grad_table, pair(1), pair(2), pair(0))


def solution(mesh):
    both = ("event", "phi")
    in_specs = (
        P(None, both),
        P(both),
        P(both, None, None, None),
        P(both, None),
        P(both),
        P(both),
        P(both),
        P(both),
        P(),
        P(),
        P(),
        P(),
        P(),
    )
    out_specs = (
        P("event"),
        P("event", None),
        P("event", None),
        P("event", None, None),
        P("event", None, None),
        P("event", None, None),
    )
    return jax.shard_map(body, mesh=mesh, in_specs=in_specs, out_specs=out_specs, check_vma=False)
```
